512 devices in a mesh: pipe: 16 (over y, core), expert: 16 (over z, x_hi), tensor: 2 (over x_lo).
Axes of the slice: x: 4 (x_hi: 2, x_lo: 2; x = x_hi * 2 + x_lo), y: 8, z: 8, core: 2. Of those that a mesh axis runs over, the one named last changes fastest.
Arguments:
- acts: bfloat16 [16, 2, 2048, 2048], P('pipe', None, 'expert', 'tensor'), may hold values from -6 to 6
- out_grad: bfloat16 [16, 2, 2048, 2048], P('pipe', None, 'expert', 'tensor'), may hold values from -4 to 4
- probs: bfloat16 [16, 2, 2048], P('pipe', None, 'expert'), may hold values from 0.099609375 to 1
- counts: int32 [16, 2, 16, 16], P('pipe', None, 'expert'), may hold values from 1 to 16, as said below
- w_gate: bfloat16 [16, 16, 1024, 512], P('pipe', 'expert', None, 'tensor'), may hold values from -0.125 to 0.125
- w_up: bfloat16 [16, 16, 1024, 512], P('pipe', 'expert', None, 'tensor'), may hold values from -0.125 to 0.125
- w_down: bfloat16 [16, 16, 512, 1024], P('pipe', 'expert', 'tensor'), may hold values from -0.25 to 0.25
Outputs:
- act_grad: bfloat16 [16, 2, 2048, 2048], P('pipe', None, 'expert', 'tensor')
- prob_grad: bfloat16 [16, 2, 2048], P('pipe', None, 'expert')
- gate_grad: bfloat16 [16, 16, 1024, 512], P('pipe', 'expert', None, 'tensor')
- up_grad: bfloat16 [16, 16, 1024, 512], P('pipe', 'expert', None, 'tensor')
- down_grad: bfloat16 [16, 16, 512, 1024], P('pipe', 'expert', 'tensor')
The draws below stay inside these ranges and needn't reach their ends.
Inputs may be any that keep to these rules, and one draw needn't show every extreme that they name: Row [p, d, s] of counts sums to 128; for each section and direction one expert gets exactly 16 rows from every source; no count exceeds 16.
All inputs are finite; a program needn't handle non-finite values.
Results may differ from the reference program's by a relative error of at most 0.008.
Values may be sent and summed in bfloat16 or wider, within the bound.
No kernel may reach another device: no remote copies, remote signals or barrier semaphores. Data moves between devices by JAX's collectives and lax.ppermute only.
A program may use at most 64 MiB of HBM per device.

```python
import jax
import jax.numpy as jnp
from jax import lax

D = 2048
FF = 512
ROWS = 128
EXPERTS = 16
CAP = 16
SECTION_ROWS = 2048
N_PIPE = 16
N_EXPERT = 16


def draw_counts(key, part):
    base_key = jax.random.fold_in(key, 7)
    others = EXPERTS - 1
    pairs = others // 2
    spread = (ROWS - CAP) // others
    extra = ROWS - CAP - spread * others
    reach = max(spread - 1, 0)
    position = jnp.arange(others, dtype=jnp.int32)
    bases = spread + (position < extra).astype(jnp.int32)

    def one_source(section, direction, source):
        group_key = jax.random.fold_in(jax.random.fold_in(base_key, section), direction)
        order = jax.random.permutation(group_key, EXPERTS).astype(jnp.int32)
        own_key = jax.random.fold_in(group_key, source + 1000)
        shifts = jax.random.randint(own_key, (pairs,), -reach, reach + 1, dtype=jnp.int32)
        moves = jnp.zeros((others,), jnp.int32).at[:pairs].add(shifts).at[pairs:2 * pairs].add(-shifts)
        values = jnp.concatenate([jnp.full((1,), CAP, jnp.int32), bases + moves])
        return jnp.zeros((EXPERTS,), jnp.int32).at[order].set(values)
    sections = jnp.arange(N_PIPE, dtype=jnp.int32)
    directions = jnp.arange(2, dtype=jnp.int32)
    sources = jnp.arange(N_EXPERT, dtype=jnp.int32)
    over_source = jax.vmap(one_source, in_axes=(None, None, 0))
    over_direction = jax.vmap(over_source, in_axes=(None, 0, None))
    over_section = jax.vmap(over_direction, in_axes=(0, None, None))
    return over_section(sections, directions, sources)


def level_of(rng, dims, pieces, smallest, largest):
    level, own = 1.0, jax.random.fold_in(rng, 6)
    for axis_at, shards_of in pieces:
        steps = jnp.exp(jax.random.uniform(jax.random.fold_in(own, axis_at), (shards_of,), jnp.float32, smallest / len(pieces), largest / len(pieces)))
        level = level * jnp.repeat(steps, dims[axis_at] // shards_of).reshape([-1 if axis == axis_at else 1 for axis in range(len(dims))])
    return level


def centred(stream_key, dims, deviation, limit, split=(), kind=jnp.bfloat16):
    gain = level_of(stream_key, dims, split, -0.22, 0.18) if split else 1.0
    result = jax.random.normal(stream_key, dims, jnp.float32) * deviation * gain
    return jnp.minimum(jnp.maximum(result, -limit), limit).astype(kind)


def setup_inputs(seed: int = 0) -> dict:
    streams_of = jax.random.split(jax.random.key(seed), 8)
    acts = centred(streams_of[0], (N_PIPE, 2, SECTION_ROWS, D), 1.0, 6.0, ((0, 16), (2, 16), (3, 2)))
    out_grad = centred(streams_of[1], (N_PIPE, 2, SECTION_ROWS, D), 0.5, 4.0, ((0, 16), (2, 16), (3, 2)))
    probs = jnp.clip(0.099609375 + 0.9003906 * jax.random.uniform(streams_of[2], (N_PIPE, 2, SECTION_ROWS), jnp.float32) ** level_of(streams_of[2], (N_PIPE, 2, SECTION_ROWS), ((0, 16), (2, 16)), -0.2, 0.2), 0.099609375, 1.0).astype(jnp.bfloat16)
    counts = draw_counts(jax.random.fold_in(streams_of[7], 71), 0)
    w_gate = centred(streams_of[4], (N_PIPE, EXPERTS, D // 2, FF), D ** -0.5, 0.125, ((0, 16), (1, 16), (3, 2)))
    w_up = centred(streams_of[5], (N_PIPE, EXPERTS, D // 2, FF), D ** -0.5, 0.125, ((0, 16), (1, 16), (3, 2)))
    w_down = centred(streams_of[6], (N_PIPE, EXPERTS, FF, D // 2), FF ** -0.5, 0.25, ((0, 16), (1, 16), (2, 2)))
    return {"acts": acts, "out_grad": out_grad, "probs": probs, "counts": counts, "w_gate": w_gate, "w_up": w_up, "w_down": w_down}


def silu_parts(gate):
    sigma = jax.nn.sigmoid(gate)
    return gate * sigma, sigma * (1.0 + gate * (1.0 - sigma))


def section_terms(section, acts, out_grad, probs, counts, w_gate, w_up, w_down):
    layers = w_gate.shape[0] // 2
    experts = counts.shape[-1]
    rows = acts.shape[2] // experts
    width = acts.shape[3]
    layer = section % layers
    count_rows = counts[section].astype(jnp.int32)
    ends = jnp.cumsum(count_rows, axis=-1).astype(jnp.int32)
    starts = (ends - count_rows).astype(jnp.int32)
    position = jnp.arange(CAP).astype(jnp.int32)
    live = position < count_rows[..., None]
    local = jnp.where(live, starts[..., None] + position, 0).astype(jnp.int32)
    dir_ids = jnp.arange(2).astype(jnp.int32)[:, None, None, None]
    src_ids = jnp.arange(experts).astype(jnp.int32)[None, :, None, None]
    global_rows = ((dir_ids * experts + src_ids) * rows + local).reshape(-1)
    live_flat = live.reshape(-1)

    def pack_rows(values):
        taken = jnp.take(values.reshape(-1, width), global_rows, axis=0)
        taken = jnp.where(live_flat[:, None], taken, jnp.zeros_like(taken))
        taken = taken.reshape(2, experts, experts, CAP, width)
        return jnp.transpose(taken, (2, 0, 1, 3, 4)).reshape(experts, -1, width)

    slots_x = pack_rows(acts[section])
    slots_g = pack_rows(out_grad[section])
    taken = jnp.take(probs[section].reshape(-1), global_rows, axis=0)
    taken = jnp.where(live_flat, taken, jnp.zeros_like(taken)).reshape(2, experts, experts, CAP)
    slots_p = jnp.transpose(taken, (2, 0, 1, 3)).reshape(experts, -1)

    full_gate = jnp.concatenate([w_gate[layer], w_gate[layer + layers]], axis=1).astype(jnp.float32)
    full_up = jnp.concatenate([w_up[layer], w_up[layer + layers]], axis=1).astype(jnp.float32)
    full_down = jnp.concatenate([w_down[layer], w_down[layer + layers]], axis=2).astype(jnp.float32)

    input_float = slots_x.astype(jnp.float32)
    grad_float = slots_g.astype(jnp.float32)
    gate = jnp.einsum('emd,edf->emf', input_float, full_gate)
    up = jnp.einsum('emd,edf->emf', input_float, full_up)
    silu_value, slope = silu_parts(gate)
    act = (silu_value * up).astype(jnp.bfloat16)
    back = jnp.einsum('emd,efd->emf', grad_float, full_down)
    prob_term = jnp.sum(act.astype(jnp.float32) * back, axis=-1)
    scale = slots_p.astype(jnp.float32)[..., None]
    d_gate = (scale * back * up * slope).astype(jnp.bfloat16)
    d_up = (scale * back * silu_value).astype(jnp.bfloat16)
    scaled = (scale * grad_float).astype(jnp.bfloat16)
    slot_grad = jnp.einsum('emf,edf->emd', d_gate.astype(jnp.float32), full_gate)
    slot_grad = slot_grad + jnp.einsum('emf,edf->emd', d_up.astype(jnp.float32), full_up)
    slot_grad = slot_grad.astype(jnp.bfloat16)
    prob_slot = prob_term.astype(jnp.bfloat16)
    section_gate = jnp.einsum('emd,emf->edf', input_float, d_gate.astype(jnp.float32)).astype(jnp.bfloat16)
    section_up = jnp.einsum('emd,emf->edf', input_float, d_up.astype(jnp.float32)).astype(jnp.bfloat16)
    section_down = jnp.einsum('emf,emd->efd', act.astype(jnp.float32), scaled.astype(jnp.float32)).astype(jnp.bfloat16)

    row_ids = jnp.arange(rows).astype(jnp.int32)
    owner = jnp.sum((ends[:, :, None, :] <= row_ids[None, None, :, None]).astype(jnp.int32), axis=-1).astype(jnp.int32)
    start_row = jnp.take_along_axis(starts, owner, axis=2).astype(jnp.int32)
    dir_two = jnp.arange(2).astype(jnp.int32)[:, None, None]
    src_two = jnp.arange(experts).astype(jnp.int32)[None, :, None]
    slot_place = (((dir_two * experts + src_two) * experts + owner) * CAP + row_ids - start_row).reshape(-1)
    grid = jnp.transpose(slot_grad.reshape(experts, 2, experts, CAP, width), (1, 2, 0, 3, 4)).reshape(-1, width)
    row_grad = jnp.take(grid, slot_place, axis=0).reshape(2, experts * rows, width)
    prob_grid = jnp.transpose(prob_slot.reshape(experts, 2, experts, CAP), (1, 2, 0, 3)).reshape(-1)
    row_prob = jnp.take(prob_grid, slot_place, axis=0).reshape(2, experts * rows)
    return row_grad, row_prob, section_gate, section_up, section_down


def combine(first, second, axis):
    total = (first.astype(jnp.float32) + second.astype(jnp.float32)).astype(jnp.bfloat16)
    half = total.shape[axis] // 2
    lower = lax.slice_in_dim(total, 0, half, axis=axis)
    higher = lax.slice_in_dim(total, half, 2 * half, axis=axis)
    return jnp.stack([lower, higher])


def reference(acts, out_grad, probs, counts, w_gate, w_up, w_down):
    layers = w_gate.shape[0] // 2

    def one_layer(layer):
        lower = section_terms(layer, acts, out_grad, probs, counts, w_gate, w_up, w_down)
        higher = section_terms(layer + layers, acts, out_grad, probs, counts, w_gate, w_up, w_down)
        row_grad = jnp.stack([lower[0], higher[0]])
        row_prob = jnp.stack([lower[1], higher[1]])
        return (row_grad, row_prob, combine(lower[2], higher[2], 1),
                combine(lower[3], higher[3], 1), combine(lower[4], higher[4], 2))

    results = lax.map(one_layer, jnp.arange(layers).astype(jnp.int32))

    def arrange(stacked):
        moved = jnp.swapaxes(stacked, 0, 1)
        return moved.reshape((2 * layers,) + stacked.shape[2:])

    return (arrange(results[0]), arrange(results[1]), arrange(results[2]),
            arrange(results[3]), arrange(results[4]))
```

```python
import jax
import jax.numpy as jnp
from jax import lax
from jax.experimental import pallas as pl
from jax.experimental.pallas import tpu as pltpu
from jax.sharding import PartitionSpec as P


BF = jnp.bfloat16
F32 = jnp.float32
VM = pl.BlockSpec(memory_space=pltpu.VMEM)
HB = pl.BlockSpec(memory_space=pltpu.HBM)


def dot(a, b, ca, cb):
    return lax.dot_general(a, b, (((ca,), (cb,)), ((), ())), preferred_element_type=F32)


def call(body, outs, args, in_specs, out_specs, scratch=(), flops=0):
    moved = sum(a.size * a.dtype.itemsize for a in (*args, *outs))
    return pl.pallas_call(
        body,
        out_shape=tuple(outs),
        in_specs=in_specs,
        out_specs=tuple(out_specs),
        scratch_shapes=scratch,
        cost_estimate=pl.CostEstimate(flops=flops, bytes_accessed=moved, transcendentals=0),
    )(*args)


def shape(dims, kind):
    return jax.ShapeDtypeStruct(dims, kind)


def slot_choice(count_row, slots, rows):
    experts = count_row.shape[1]
    total = experts * slots
    owner = lax.broadcasted_iota(jnp.int32, (total, experts), 0) // slots
    expert = lax.broadcasted_iota(jnp.int32, (total, experts), 1)
    count = jnp.sum(jnp.where(expert == owner, count_row, 0), axis=1, keepdims=True)
    start = jnp.sum(jnp.where(expert < owner, count_row, 0), axis=1, keepdims=True)
    place = lax.broadcasted_iota(jnp.int32, (total, 1), 0) % slots
    target = jnp.where(place < count, start + place, -1)
    return lax.broadcasted_iota(jnp.int32, (total, rows), 1) == target


def pack_body(counts_ref, values_ref, out_ref):
    dirs, rows, width = values_ref.shape
    experts, _, slots, _ = out_ref.shape
    for d in range(dirs):
        mask = slot_choice(counts_ref[d : d + 1, :], slots, rows)
        packed = dot(mask.astype(BF), values_ref[d], 1, 0).astype(BF)
        out_ref[:, d] = packed.reshape(experts, slots, width)


def pack_scaled_body(counts_ref, probs_ref, values_ref, out_ref):
    dirs, rows, width = values_ref.shape
    experts, _, slots, _ = out_ref.shape
    for d in range(dirs):
        mask = slot_choice(counts_ref[d : d + 1, :], slots, rows)
        weight = jnp.where(mask, probs_ref[d : d + 1, :].astype(F32), 0.0).astype(BF)
        packed = dot(weight, values_ref[d], 1, 0).astype(BF)
        out_ref[:, d] = packed.reshape(experts, slots, width)


def unpack_body(counts_ref, slots_ref, out_ref):
    experts, dirs, slots, width = slots_ref.shape
    rows = out_ref.shape[1]
    for d in range(dirs):
        mask = slot_choice(counts_ref[d : d + 1, :], slots, rows)
        filled = slots_ref[:, d].reshape(experts * slots, width)
        out_ref[d] = dot(mask.astype(BF), filled, 0, 0).astype(BF)


def unpack_prob_body(counts_ref, probs_ref, own_ref, other_ref, out_ref):
    dirs, rows = out_ref.shape
    experts = own_ref.shape[0]
    total = own_ref[:, 0, :] + other_ref[:, 0, :]
    slots = 2 * rows // experts
    row = lax.broadcasted_iota(jnp.int32, (slots, rows), 1)
    place = lax.broadcasted_iota(jnp.int32, (slots, rows), 0)
    for d in range(dirs):
        found = jnp.zeros((slots, rows), F32)
        start = jnp.zeros((1, 1), jnp.int32)
        for e in range(experts):
            count = counts_ref[d : d + 1, e : e + 1]
            here = (row - start == place) & (place < count)
            values = total[e : e + 1, d * slots : (d + 1) * slots].reshape(slots, 1)
            found = jnp.where(here, values, found)
            start = start + count
        summed = jnp.sum(found, axis=0, keepdims=True)
        out_ref[d : d + 1, :] = (summed / probs_ref[d : d + 1, :].astype(F32)).astype(BF)


def half_index():
    return lax.axis_index("pipe") // (lax.axis_size("pipe") // 2)


def load(copies):
    for c in copies:
        c.start()
    for c in copies:
        c.wait()


def hidden_body(own, other, wg, wgo, wu, wuo, act_ref, silu_ref, slope_ref, xs, ws, sems):
    same = (lax.axis_index("tensor") == half_index()).astype(jnp.int32)
    load([
        pltpu.make_async_copy(own, xs.at[1 - same], sems.at[0]),
        pltpu.make_async_copy(other, xs.at[same], sems.at[1]),
        pltpu.make_async_copy(wg, ws.at[0], sems.at[2]),
        pltpu.make_async_copy(wgo, ws.at[1], sems.at[3]),
        pltpu.make_async_copy(wu, ws.at[2], sems.at[4]),
        pltpu.make_async_copy(wuo, ws.at[3], sems.at[5]),
    ])
    gate = dot(xs[0], ws[0], 1, 0) + dot(xs[1], ws[1], 1, 0)
    up = dot(xs[0], ws[2], 1, 0) + dot(xs[1], ws[3], 1, 0)
    sigma = jax.nn.sigmoid(gate)
    silu = gate * sigma
    act_ref[...] = (silu * up).astype(BF)
    silu_ref[...] = silu
    slope_ref[...] = up * (sigma * (1.0 + gate * (1.0 - sigma)))


def slope_body(
    own, other, wd, wdo, xown, xother, act, silu, slope,
    dg_ref, du_ref, prob_ref, down_ref, gate_ref, up_ref,
    gs, xs, ws, sems,
):
    same = (lax.axis_index("tensor") == half_index()).astype(jnp.int32)

    @pl.when(same == 1)
    def _():
        pltpu.make_async_copy(xother, xs, sems.at[4]).start()

    @pl.when(same == 0)
    def _():
        pltpu.make_async_copy(xown, xs, sems.at[4]).start()

    load([
        pltpu.make_async_copy(own, gs.at[1 - same], sems.at[0]),
        pltpu.make_async_copy(other, gs.at[same], sems.at[1]),
        pltpu.make_async_copy(wd, ws.at[0], sems.at[2]),
        pltpu.make_async_copy(wdo, ws.at[1], sems.at[3]),
    ])
    pltpu.make_async_copy(xown, xs, sems.at[4]).wait()
    back = dot(gs[0], ws[0], 1, 1) + dot(gs[1], ws[1], 1, 1)
    hidden = act[...]
    dg = (back * slope[...]).astype(BF)
    du = (back * silu[...]).astype(BF)
    dg_ref[...] = dg
    du_ref[...] = du
    term = hidden.astype(F32) * back
    high = term.astype(BF)
    low = (term - high.astype(F32)).astype(BF)
    ones = jnp.ones((8, term.shape[1]), BF)
    prob = dot(ones, high, 1, 1) + dot(ones, low, 1, 1)
    blocks = prob_ref.shape[0]
    width = prob.shape[1] // blocks
    prob_ref[...] = jnp.zeros_like(prob_ref)
    for s in range(blocks):
        prob_ref[s, :, 0:width] = prob[:, s * width : (s + 1) * width]
    down_ref[...] = dot(hidden, gs[1], 0, 0).astype(BF)
    gate_ref[...] = dot(xs[...], dg, 0, 0).astype(BF)
    up_ref[...] = dot(xs[...], du, 0, 0).astype(BF)


def input_body(dg, du, wg, wgo, wu, wuo, keep_ref, send_ref, ws, sems):
    same = (lax.axis_index("tensor") == half_index()).astype(jnp.int32)
    load([
        pltpu.make_async_copy(wg, ws.at[1 - same], sems.at[0]),
        pltpu.make_async_copy(wgo, ws.at[same], sems.at[1]),
        pltpu.make_async_copy(wu, ws.at[3 - same], sems.at[2]),
        pltpu.make_async_copy(wuo, ws.at[2 + same], sems.at[3]),
    ])
    send_ref[...] = (dot(dg[...], ws[1], 1, 1) + dot(du[...], ws[3], 1, 1)).astype(BF)
    keep_ref[...] = dot(dg[...], ws[0], 1, 1) + dot(du[...], ws[2], 1, 1)


def keep_body(own, other, xown, xother, act, dg, du, gate_ref, up_ref, down_ref, xs, gs, sems):
    same = lax.axis_index("tensor") == half_index()

    @pl.when(same)
    def _():
        pltpu.make_async_copy(xown, xs, sems.at[0]).start()
        pltpu.make_async_copy(own, gs, sems.at[1]).start()

    @pl.when(jnp.logical_not(same))
    def _():
        pltpu.make_async_copy(xother, xs, sems.at[0]).start()
        pltpu.make_async_copy(other, gs, sems.at[1]).start()

    pltpu.make_async_copy(xown, xs, sems.at[0]).wait()
    pltpu.make_async_copy(own, gs, sems.at[1]).wait()
    gate_ref[...] = dot(xs[...], dg[...], 0, 0)
    up_ref[...] = dot(xs[...], du[...], 0, 0)
    down_ref[...] = dot(act[...], gs[...], 0, 0)


def settle(keep, arrived):
    return (keep + arrived.astype(F32)).astype(BF)[None, None]


def on_device(acts, out_grad, probs, counts, w_gate, w_up, w_down):
    experts = lax.axis_size("expert")
    pipes = lax.axis_size("pipe")
    dirs, rows, width = acts.shape[1:]
    slots = 2 * rows // experts
    total = dirs * experts * slots
    hidden = w_gate.shape[3]
    mirror = [(i, (i + pipes // 2) % pipes) for i in range(pipes)]
    swap = [(0, 1), (1, 0)]
    count_rows = counts[0, :, 0, :]
    wg, wu, wd = (w_gate[0, 0], w_up[0, 0], w_down[0, 0])
    packed = shape((experts, dirs, slots, width), BF)
    work = 2 * dirs * experts * slots * rows * width

    (x_send,) = call(pack_body, [packed], (count_rows, acts[0]), [VM, VM], [VM], flops=work)
    (g_send,) = call(
        pack_scaled_body, [packed], (count_rows, probs[0], out_grad[0]), [VM, VM, VM], [VM], flops=work
    )
    x_own = lax.all_to_all(x_send, "expert", 0, 0, tiled=True).reshape(total, width)
    g_own = lax.all_to_all(g_send, "expert", 0, 0, tiled=True).reshape(total, width)
    wgo = lax.ppermute(wg, "pipe", mirror)
    wuo = lax.ppermute(wu, "pipe", mirror)
    wdo = lax.ppermute(wd, "pipe", mirror)
    x_other = lax.ppermute(x_own, "tensor", swap)
    g_other = lax.ppermute(g_own, "tensor", swap)

    sems = pltpu.SemaphoreType.DMA
    one = 2 * total * width * hidden
    act, silu, slope = call(
        hidden_body,
        [shape((total, hidden), BF), shape((total, hidden), F32), shape((total, hidden), F32)],
        (x_own, x_other, wg, wgo, wu, wuo),
        [HB] * 6,
        [VM] * 3,
        [pltpu.VMEM((2, total, width), BF), pltpu.VMEM((4, width, hidden), BF), sems((6,))],
        4 * one,
    )
    dg, du, prob, down_send, gate_send, up_send = call(
        slope_body,
        [
            shape((total, hidden), BF),
            shape((total, hidden), BF),
            shape((experts, 8, 128), F32),
            shape((hidden, width), BF),
            shape((width, hidden), BF),
            shape((width, hidden), BF),
        ],
        (g_own, g_other, wd, wdo, x_own, x_other, act, silu, slope),
        [HB] * 6 + [VM] * 3,
        [VM] * 6,
        [
            pltpu.VMEM((2, total, width), BF),
            pltpu.VMEM((total, width), BF),
            pltpu.VMEM((2, hidden, width), BF),
            sems((5,)),
        ],
        5 * one,
    )
    down_got = lax.ppermute(down_send, "pipe", mirror)
    gate_got = lax.ppermute(gate_send, "pipe", mirror)
    up_got = lax.ppermute(up_send, "pipe", mirror)
    row_keep, row_send = call(
        input_body,
        [shape((total, width), F32), shape((total, width), BF)],
        (dg, du, wg, wgo, wu, wuo),
        [VM] * 2 + [HB] * 4,
        [VM] * 2,
        [pltpu.VMEM((4, width, hidden), BF), sems((4,))],
        4 * one,
    )
    row_got = lax.ppermute(row_send, "tensor", swap)
    prob_own = lax.all_to_all(prob, "expert", 0, 0, tiled=True)
    prob_other = lax.ppermute(prob_own, "tensor", swap)
    gate_keep, up_keep, down_keep = call(
        keep_body,
        [shape((width, hidden), F32), shape((width, hidden), F32), shape((hidden, width), F32)],
        (g_own, g_other, x_own, x_other, act, dg, du),
        [HB] * 4 + [VM] * 3,
        [VM] * 3,
        [pltpu.VMEM((total, width), BF), pltpu.VMEM((total, width), BF), sems((2,))],
        3 * one,
    )
    (prob_grad,) = call(
        unpack_prob_body,
        [shape((dirs, rows), BF)],
        (count_rows, probs[0], prob_own, prob_other),
        [VM] * 4,
        [VM],
    )
    row_sum = (row_keep + row_got.astype(F32)).astype(BF).reshape(experts, dirs, slots, width)
    row_back = lax.all_to_all(row_sum, "expert", 0, 0, tiled=True)
    (act_grad,) = call(
        unpack_body, [shape((dirs, rows, width), BF)], (count_rows, row_back), [VM, VM], [VM], flops=work
    )
    return (
        act_grad[None],
        prob_grad[None],
        settle(gate_keep, gate_got),
        settle(up_keep, up_got),
        settle(down_keep, down_got),
    )


def solution(mesh):
    return jax.shard_map(
        on_device,
        mesh=mesh,
        in_specs=(
            P("pipe", None, "expert", "tensor"),
            P("pipe", None, "expert", "tensor"),
            P("pipe", None, "expert"),
            P("pipe", None, "expert", None),
            P("pipe", "expert", None, "tensor"),
            P("pipe", "expert", None, "tensor"),
            P("pipe", "expert", "tensor", None),
        ),
        out_specs=(
            P("pipe", None, "expert", "tensor"),
            P("pipe", None, "expert"),
            P("pipe", "expert", None, "tensor"),
            P("pipe", "expert", None, "tensor"),
            P("pipe", "expert", "tensor", None),
        ),
        check_vma=False,
    )
```

```python
import jax
import jax.numpy as jnp
from jax import lax
from jax.experimental import pallas as pl
from jax.experimental.pallas import tpu as pltpu
from jax.sharding import PartitionSpec as P


BF = jnp.bfloat16
F32 = jnp.float32
VM = pl.BlockSpec(memory_space=pltpu.VMEM)


def dot(a, b, ca, cb):
    return lax.dot_general(a, b, (((ca,), (cb,)), ((), ())), preferred_element_type=F32)


def call(body, outs, args, in_specs, out_specs, scratch=(), flops=0):
    moved = sum(a.size * a.dtype.itemsize for a in (*args, *outs))
    return pl.pallas_call(
        body,
        out_shape=tuple(outs),
        in_specs=in_specs,
        out_specs=tuple(out_specs),
        scratch_shapes=scratch,
        cost_estimate=pl.CostEstimate(flops=flops, bytes_accessed=moved, transcendentals=0),
    )(*args)


def shape(dims, kind):
    return jax.ShapeDtypeStruct(dims, kind)


def slot_choice(count_row, slots, rows):
    experts = count_row.shape[1]
    total = experts * slots
    owner = lax.broadcasted_iota(jnp.int32, (total, experts), 0) // slots
    expert = lax.broadcasted_iota(jnp.int32, (total, experts), 1)
    count = jnp.sum(jnp.where(expert == owner, count_row, 0), axis=1, keepdims=True)
    start = jnp.sum(jnp.where(expert < owner, count_row, 0), axis=1, keepdims=True)
    place = lax.broadcasted_iota(jnp.int32, (total, 1), 0) % slots
    target = jnp.where(place < count, start + place, -1)
    return lax.broadcasted_iota(jnp.int32, (total, rows), 1) == target


def pack_body(counts_ref, values_ref, out_ref):
    dirs, rows, width = values_ref.shape
    experts, _, slots, _ = out_ref.shape
    for d in range(dirs):
        mask = slot_choice(counts_ref[d : d + 1, :], slots, rows)
        packed = dot(mask.astype(BF), values_ref[d], 1, 0).astype(BF)
        out_ref[:, d] = packed.reshape(experts, slots, width)


def pack_scaled_body(counts_ref, probs_ref, values_ref, out_ref):
    dirs, rows, width = values_ref.shape
    experts, _, slots, _ = out_ref.shape
    for d in range(dirs):
        mask = slot_choice(counts_ref[d : d + 1, :], slots, rows)
        weight = jnp.where(mask, probs_ref[d : d + 1, :].astype(F32), 0.0).astype(BF)
        packed = dot(weight, values_ref[d], 1, 0).astype(BF)
        out_ref[:, d] = packed.reshape(experts, slots, width)


def unpack_body(counts_ref, slots_ref, out_ref):
    experts, dirs, slots, width = slots_ref.shape
    rows = out_ref.shape[1]
    for d in range(dirs):
        mask = slot_choice(counts_ref[d : d + 1, :], slots, rows)
        filled = slots_ref[:, d].reshape(experts * slots, width)
        out_ref[d] = dot(mask.astype(BF), filled, 0, 0).astype(BF)


def unpack_prob_body(counts_ref, probs_ref, own_ref, other_ref, out_ref):
    dirs, rows = out_ref.shape
    experts = own_ref.shape[0]
    total = own_ref[:, 0, :] + other_ref[:, 0, :]
    slots = 2 * rows // experts
    row = lax.broadcasted_iota(jnp.int32, (slots, rows), 1)
    place = lax.broadcasted_iota(jnp.int32, (slots, rows), 0)
    for d in range(dirs):
        found = jnp.zeros((slots, rows), F32)
        start = jnp.zeros((1, 1), jnp.int32)
        for e in range(experts):
            count = counts_ref[d : d + 1, e : e + 1]
            here = (row - start == place) & (place < count)
            values = total[e : e + 1, d * slots : (d + 1) * slots].reshape(slots, 1)
            found = jnp.where(here, values, found)
            start = start + count
        summed = jnp.sum(found, axis=0, keepdims=True)
        out_ref[d : d + 1, :] = (summed / probs_ref[d : d + 1, :].astype(F32)).astype(BF)


def keeps_low():
    half = lax.axis_index("pipe") // (lax.axis_size("pipe") // 2)
    group = (lax.axis_index("tensor") + lax.axis_index("expert")) % 2
    return half == group


def sides(own_ref, other_ref):
    blocks, _, rows, width = own_ref.shape

    def rows_of(ref, side):
        return ref[:, side].reshape(blocks * rows, width)

    return (
        jnp.concatenate([rows_of(own_ref, 0), rows_of(other_ref, 1)], axis=0),
        jnp.concatenate([rows_of(other_ref, 0), rows_of(own_ref, 1)], axis=0),
    )


def weight_sides(same, own_ref, other_ref):
    own, other = (own_ref[...], other_ref[...])
    return (jnp.where(same, own, other), jnp.where(same, other, own))


def hidden_body(own, other, wg, wgo, wu, wuo, act_ref, act_t_ref, silu_ref, slope_ref, send_ref, keep_ref):
    same = keeps_low()
    xa, xb = sides(own, other)
    wga, wgb = weight_sides(same, wg, wgo)
    wua, wub = weight_sides(same, wu, wuo)
    gate = dot(xa, wga, 1, 0) + dot(xb, wgb, 1, 0)
    up = dot(xa, wua, 1, 0) + dot(xb, wub, 1, 0)
    sigma = jax.nn.sigmoid(gate)
    silu = gate * sigma
    act = (silu * up).astype(BF)
    act_ref[...] = act
    act_t_ref[...] = act.T
    silu_ref[...] = silu
    slope_ref[...] = up * (sigma * (1.0 + gate * (1.0 - sigma)))
    send_ref[...] = jnp.where(same, xb, xa).T
    keep_ref[...] = jnp.where(same, xa, xb).T


def slope_body(own, other, wd, wdo, act, act_t, silu, slope, d_ref, prob_ref, down_ref):
    same = keeps_low()
    ga, gb = sides(own, other)
    wda, wdb = weight_sides(same, wd, wdo)
    down_ref[...] = dot(act_t[...], jnp.where(same, gb, ga), 1, 0).astype(BF)
    back = dot(ga, wda, 1, 1) + dot(gb, wdb, 1, 1)
    hidden = back.shape[1]
    d_ref[:, 0:hidden] = (back * slope[...]).astype(BF)
    d_ref[:, hidden : 2 * hidden] = (back * silu[...]).astype(BF)
    term = act[...].astype(F32) * back
    high = term.astype(BF)
    low = (term - high.astype(F32)).astype(BF)
    ones = jnp.ones((8, hidden), BF)
    prob = dot(ones, high, 1, 1) + dot(ones, low, 1, 1)
    blocks = prob_ref.shape[0]
    width = prob.shape[1] // blocks
    prob_ref[...] = jnp.zeros_like(prob_ref)
    for i in range(blocks):
        side, z = divmod(i, blocks // 2)
        prob_ref[2 * z + side, :, 0:width] = prob[:, i * width : (i + 1) * width]


def row_terms(d, wg, wgo, wu, wuo, out_ref, swapped):
    wga, wgb = weight_sides(keeps_low(), wg, wgo)
    wua, wub = weight_sides(keeps_low(), wu, wuo)
    blocks, _, rows, width = out_ref.shape
    half = blocks * rows
    hidden = wga.shape[1]
    for side in range(2):
        first = side == (1 if swapped else 0)
        part = pl.ds(side * half, half)
        term = dot(d[part, 0:hidden], wga if first else wgb, 1, 1)
        term = term + dot(d[part, hidden : 2 * hidden], wua if first else wub, 1, 1)
        out_ref[:, side] = term.astype(out_ref.dtype).reshape(blocks, rows, width)


def row_send_body(d, wg, wgo, wu, wuo, out_ref):
    row_terms(d, wg, wgo, wu, wuo, out_ref, True)


def grad_send_body(x_t, d, out_ref):
    both = dot(x_t[...], d[...], 1, 0).astype(BF)
    hidden = out_ref.shape[2]
    out_ref[0] = both[:, :hidden]
    out_ref[1] = both[:, hidden:]


def keep_body(own, other, x_t, act_t, d, wg, wgo, wu, wuo, row_ref, grad_ref, down_ref):
    row_terms(d, wg, wgo, wu, wuo, row_ref, False)
    ga, gb = sides(own, other)
    both = dot(x_t[...], d[...], 1, 0)
    hidden = grad_ref.shape[2]
    grad_ref[0] = both[:, :hidden]
    grad_ref[1] = both[:, hidden:]
    down_ref[...] = dot(act_t[...], jnp.where(keeps_low(), ga, gb), 1, 0)


def dispatch(array):
    experts = lax.axis_size("expert")
    groups = [[2 * e + (e + g) % 2 for e in range(experts)] for g in range(2)]
    return lax.all_to_all(
        array, ("expert", "tensor"), 0, 0, axis_index_groups=groups, tiled=True
    )


def settle(keep, arrived):
    return (keep + arrived.astype(F32)).astype(BF)[None, None]


def on_device(acts, out_grad, probs, counts, w_gate, w_up, w_down):
    experts = lax.axis_size("expert")
    pipes = lax.axis_size("pipe")
    dirs, rows, width = acts.shape[1:]
    slots = 2 * rows // experts
    total = dirs * experts * slots
    hidden = w_gate.shape[3]
    wg, wu, wd = (w_gate[0, 0], w_up[0, 0], w_down[0, 0])
    count_rows = counts[0, :, 0, :]
    packed = shape((experts, dirs, slots, width), BF)
    sided = shape((experts // 2, 2, dirs * slots, width), BF)
    work = 2 * dirs * experts * slots * rows * width
    one = 2 * total * width * hidden

    def mirror(array):
        return lax.ppermute(array, "pipe", [(i, (i + pipes // 2) % pipes) for i in range(pipes)])

    def swap(array):
        return lax.ppermute(array, "tensor", [(0, 1), (1, 0)])

    def kernel(body, outs, args, flops):
        return call(body, outs, args, [VM] * len(args), [VM] * len(outs), (), flops)

    (x_send,) = kernel(pack_body, [packed], (count_rows, acts[0]), work)
    x_own = dispatch(x_send).reshape(sided.shape)
    wgo = mirror(wg)
    (g_send,) = kernel(pack_scaled_body, [packed], (count_rows, probs[0], out_grad[0]), work)
    g_own = dispatch(g_send).reshape(sided.shape)
    wuo = mirror(wu)
    wdo = mirror(wd)
    x_other = swap(x_own)
    g_other = swap(g_own)
    act, act_t, silu, slope, x_send_t, x_keep_t = kernel(
        hidden_body,
        [
            shape((total, hidden), BF),
            shape((hidden, total), BF),
            shape((total, hidden), F32),
            shape((total, hidden), F32),
            shape((width, total), BF),
            shape((width, total), BF),
        ],
        (x_own, x_other, wg, wgo, wu, wuo),
        4 * one,
    )
    d, prob, down_send = kernel(
        slope_body,
        [shape((total, 2 * hidden), BF), shape((experts, 8, 128), F32), shape((hidden, width), BF)],
        (g_own, g_other, wd, wdo, act, act_t, silu, slope),
        3 * one,
    )
    down_got = mirror(down_send)
    (row_send,) = kernel(row_send_body, [sided], (d, wg, wgo, wu, wuo), 2 * one)
    row_got = swap(row_send)
    (grad_send,) = kernel(grad_send_body, [shape((2, width, hidden), BF)], (x_send_t, d), 2 * one)
    grad_got = mirror(grad_send)
    prob_own = dispatch(prob)
    row_keep, grad_keep, down_keep = kernel(
        keep_body,
        [shape(sided.shape, F32), shape((2, width, hidden), F32), shape((hidden, width), F32)],
        (g_own, g_other, x_keep_t, act_t, d, wg, wgo, wu, wuo),
        5 * one,
    )
    prob_other = swap(prob_own)
    row_sum = (row_keep + row_got.astype(F32)).astype(BF).reshape(packed.shape)
    row_back = dispatch(row_sum)
    (prob_grad,) = kernel(
        unpack_prob_body, [shape((dirs, rows), BF)], (count_rows, probs[0], prob_own, prob_other), 0
    )
    (act_grad,) = kernel(
        unpack_body, [shape((dirs, rows, width), BF)], (count_rows, row_back), work
    )
    return (
        act_grad[None],
        prob_grad[None],
        settle(grad_keep[0], grad_got[0]),
        settle(grad_keep[1], grad_got[1]),
        settle(down_keep, down_got),
    )


def solution(mesh):
    return jax.shard_map(
        on_device,
        mesh=mesh,
        in_specs=(
            P("pipe", None, "expert", "tensor"),
            P("pipe", None, "expert", "tensor"),
            P("pipe", None, "expert"),
            P("pipe", None, "expert", None),
            P("pipe", "expert", None, "tensor"),
            P("pipe", "expert", None, "tensor"),
            P("pipe", "expert", "tensor", None),
        ),
        out_specs=(
            P("pipe", None, "expert", "tensor"),
            P("pipe", None, "expert"),
            P("pipe", "expert", None, "tensor"),
            P("pipe", "expert", None, "tensor"),
            P("pipe", "expert", "tensor", None),
        ),
        check_vma=False,
    )
```

```python
import jax
import jax.numpy as jnp
from jax import lax
from jax.experimental import pallas as pl
from jax.experimental.pallas import tpu as pltpu
from jax.sharding import PartitionSpec as P


BF = jnp.bfloat16
F32 = jnp.float32
VM = pl.BlockSpec(memory_space=pltpu.VMEM)
ANY = pl.BlockSpec(memory_space=pl.ANY)
LANES = 128


def dot(a, b, ca, cb):
    return lax.dot_general(a, b, (((ca,), (cb,)), ((), ())), preferred_element_type=F32)


def call(body, outs, args, in_specs, out_specs, scratch=(), flops=0, limit=None):
    moved = sum(a.size * a.dtype.itemsize for a in (*args, *outs))
    return pl.pallas_call(
        body,
        out_shape=tuple(outs),
        in_specs=in_specs,
        out_specs=tuple(out_specs),
        scratch_shapes=scratch,
        compiler_params=pltpu.CompilerParams(vmem_limit_bytes=limit),
        cost_estimate=pl.CostEstimate(flops=flops, bytes_accessed=moved, transcendentals=0),
    )(*args)


def shape(dims, kind):
    return jax.ShapeDtypeStruct(dims, kind)


def slot_choice(count_row, slots, rows):
    experts = count_row.shape[1]
    total = experts * slots
    owner = lax.broadcasted_iota(jnp.int32, (total, experts), 0) // slots
    expert = lax.broadcasted_iota(jnp.int32, (total, experts), 1)
    count = jnp.sum(jnp.where(expert == owner, count_row, 0), axis=1, keepdims=True)
    start = jnp.sum(jnp.where(expert < owner, count_row, 0), axis=1, keepdims=True)
    place = lax.broadcasted_iota(jnp.int32, (total, 1), 0) % slots
    target = jnp.where(place < count, start + place, -1)
    return lax.broadcasted_iota(jnp.int32, (total, rows), 1) == target


def pack_body(counts_ref, values_ref, out_ref):
    dirs, rows, width = values_ref.shape
    experts, _, slots, _ = out_ref.shape
    for d in range(dirs):
        mask = slot_choice(counts_ref[d : d + 1, :], slots, rows)
        packed = dot(mask.astype(BF), values_ref[d], 1, 0).astype(BF)
        out_ref[:, d] = packed.reshape(experts, slots, width)


def pack_scaled_body(counts_ref, probs_ref, values_ref, out_ref):
    dirs, rows, width = values_ref.shape
    experts, _, slots, _ = out_ref.shape
    for d in range(dirs):
        mask = slot_choice(counts_ref[d : d + 1, :], slots, rows)
        weight = jnp.where(mask, probs_ref[d : d + 1, :].astype(F32), 0.0).astype(BF)
        packed = dot(weight, values_ref[d], 1, 0).astype(BF)
        out_ref[:, d] = packed.reshape(experts, slots, width)


def unpack_body(counts_ref, probs_ref, filled, out_ref, prob_ref, slots_ref, sem):
    copy = pltpu.make_async_copy(filled, slots_ref, sem)
    copy.start()
    experts, slots, _ = slots_ref.shape
    dirs, rows, width = out_ref.shape
    masks = [
        slot_choice(counts_ref[d : d + 1, :], slots, rows).astype(BF) for d in range(dirs)
    ]
    copy.wait()
    terms = slots_ref[:, :, dirs * width :].reshape(experts * slots, LANES)
    for d in range(dirs):
        part = slots_ref[:, :, d * width : (d + 1) * width].reshape(experts * slots, width)
        out_ref[d] = dot(masks[d], part, 0, 0).astype(BF)
        found = dot(terms, masks[d], 0, 0)[d : d + 1, :]
        prob_ref[d : d + 1, :] = (found / probs_ref[d : d + 1, :].astype(F32)).astype(BF)


def keeps_low():
    half = lax.axis_index("pipe") // (lax.axis_size("pipe") // 2)
    group = (lax.axis_index("tensor") + lax.axis_index("expert")) % 2
    return half == group


def row_copies(own, other, low, high, sems):
    return [
        pltpu.make_async_copy(own.at[:, 0], low.at[0], sems.at[0]),
        pltpu.make_async_copy(other.at[:, 1], low.at[1], sems.at[1]),
        pltpu.make_async_copy(other.at[:, 0], high.at[0], sems.at[2]),
        pltpu.make_async_copy(own.at[:, 1], high.at[1], sems.at[3]),
    ]


def flat(ref):
    sides, blocks, rows, width = ref.shape
    return ref[...].reshape(sides * blocks * rows, width)


def weight_sides(same, own_ref, other_ref):
    own, other = (own_ref[...], other_ref[...])
    return (jnp.where(same, own, other), jnp.where(same, other, own))


def hidden_body(
    own, other, wg, wgo, wu, wuo, act_ref, act_t_ref, silu_ref, slope_ref, send_ref, keep_ref, low, high, sems
):
    copies = row_copies(own, other, low, high, sems)
    for c in copies:
        c.start()
    same = keeps_low()
    wga, wgb = weight_sides(same, wg, wgo)
    wua, wub = weight_sides(same, wu, wuo)
    for c in copies:
        c.wait()
    xa, xb = (flat(low), flat(high))
    gate = dot(xa, wga, 1, 0) + dot(xb, wgb, 1, 0)
    up = dot(xa, wua, 1, 0) + dot(xb, wub, 1, 0)
    sigma = jax.nn.sigmoid(gate)
    silu = gate * sigma
    act = (silu * up).astype(BF)
    act_ref[...] = act
    act_t_ref[...] = act.T
    silu_ref[...] = silu
    slope_ref[...] = up * (sigma * (1.0 + gate * (1.0 - sigma)))
    send_ref[...] = jnp.where(same, xb, xa).T
    keep_ref[...] = jnp.where(same, xa, xb).T


def half_copies(own, other, wanted_low, buffer, sems):
    @pl.when(wanted_low)
    def _():
        pltpu.make_async_copy(own.at[:, 0], buffer.at[0], sems.at[0]).start()
        pltpu.make_async_copy(other.at[:, 1], buffer.at[1], sems.at[1]).start()

    @pl.when(jnp.logical_not(wanted_low))
    def _():
        pltpu.make_async_copy(other.at[:, 0], buffer.at[0], sems.at[0]).start()
        pltpu.make_async_copy(own.at[:, 1], buffer.at[1], sems.at[1]).start()

    return [
        pltpu.make_async_copy(own.at[:, 0], buffer.at[0], sems.at[0]),
        pltpu.make_async_copy(own.at[:, 1], buffer.at[1], sems.at[1]),
    ]


def down_body(own, other, act_t, down_ref, half, sems):
    for c in half_copies(own, other, jnp.logical_not(keeps_low()), half, sems):
        c.wait()
    down_ref[...] = dot(act_t[...], flat(half), 1, 0).astype(BF)


def row_terms(d, gate_sides, up_sides, prob, out_ref, swapped):
    blocks, _, slots, lanes = out_ref.shape
    width = gate_sides[0].shape[0]
    dirs = lanes // width
    half = blocks * dirs * slots
    hidden = gate_sides[0].shape[1]
    lane = lax.broadcasted_iota(jnp.int32, (blocks, slots, LANES), 2)
    for side in range(2):
        use = side ^ swapped
        part = d[side * half : (side + 1) * half]
        term = dot(part[:, :hidden], gate_sides[use], 1, 1) + dot(part[:, hidden:], up_sides[use], 1, 1)
        term = term.astype(out_ref.dtype).reshape(blocks, dirs, slots, width)
        spread = jnp.broadcast_to(prob[side * half : (side + 1) * half], (half, LANES))
        spread = spread.reshape(blocks, dirs, slots, LANES)
        extra = jnp.zeros((blocks, slots, LANES), F32)
        for k in range(dirs):
            out_ref[:, side, :, k * width : (k + 1) * width] = term[:, k]
            extra = jnp.where(lane == k, spread[:, k], extra)
        out_ref[:, side, :, dirs * width :] = extra.astype(out_ref.dtype)


def slope_body(
    own, other, wd, wdo, act, silu, slope, wg, wgo, wu, wuo, d_ref, prob_ref, row_ref, low, high, sems
):
    copies = row_copies(own, other, low, high, sems)
    for c in copies:
        c.start()
    same = keeps_low()
    wda, wdb = weight_sides(same, wd, wdo)
    for c in copies:
        c.wait()
    back = dot(flat(low), wda, 1, 1) + dot(flat(high), wdb, 1, 1)
    d_gate = (back * slope[...]).astype(BF)
    d_up = (back * silu[...]).astype(BF)
    d = jnp.concatenate([d_gate, d_up], axis=1)
    d_ref[...] = d
    prob = jnp.sum(act[...].astype(F32) * back, axis=1, keepdims=True)
    prob_ref[...] = jnp.broadcast_to(prob, prob_ref.shape)
    row_terms(d, weight_sides(same, wg, wgo), weight_sides(same, wu, wuo), prob, row_ref, 1)


def grad_send_body(x_t, d, out_ref):
    both = dot(x_t[...], d[...], 1, 0).astype(BF)
    hidden = out_ref.shape[2]
    out_ref[0] = both[:, :hidden]
    out_ref[1] = both[:, hidden:]


def keep_body(
    own, other, x_t, act_t, d, prob, wg, wgo, wu, wuo, row_ref, grad_ref, down_ref, half, sems
):
    same = keeps_low()
    waits = half_copies(own, other, same, half, sems)
    row_terms(
        d[...], weight_sides(same, wg, wgo), weight_sides(same, wu, wuo), prob[:, 0:1], row_ref, 0
    )
    both = dot(x_t[...], d[...], 1, 0)
    hidden = grad_ref.shape[2]
    grad_ref[0] = both[:, :hidden]
    grad_ref[1] = both[:, hidden:]
    for c in waits:
        c.wait()
    down_ref[...] = dot(act_t[...], flat(half), 1, 0)


def dispatch(array):
    experts = lax.axis_size("expert")
    groups = [[2 * e + (e + g) % 2 for e in range(experts)] for g in range(2)]
    return lax.all_to_all(
        array, ("expert", "tensor"), 0, 0, axis_index_groups=groups, tiled=True
    )


def settle(keep, arrived):
    return (keep + arrived.astype(F32)).astype(BF)[None, None]


def on_device(acts, out_grad, probs, counts, w_gate, w_up, w_down):
    experts = lax.axis_size("expert")
    pipes = lax.axis_size("pipe")
    dirs, rows, width = acts.shape[1:]
    slots = 2 * rows // experts
    total = dirs * experts * slots
    hidden = w_gate.shape[3]
    wg, wu, wd = (w_gate[0, 0], w_up[0, 0], w_down[0, 0])
    count_rows = counts[0, :, 0, :]
    packed = shape((experts, dirs, slots, width), BF)
    sided = shape((experts // 2, 2, dirs * slots, width), BF)
    work = 2 * dirs * experts * slots * rows * width
    one = 2 * total * width * hidden

    def mirror(array):
        return lax.ppermute(array, "pipe", [(i, (i + pipes // 2) % pipes) for i in range(pipes)])

    def swap(array):
        return lax.ppermute(array, "tensor", [(0, 1), (1, 0)])

    late = ("down", "slope", "gradsend", "keep", "unpack")

    def kernel(name, body, outs, args, flops, in_place=(), scratch=()):
        limit = 24 * 1024 * 1024 if name in late else None
        specs = [ANY if i in in_place else VM for i in range(len(args))]
        return call(body, outs, args, specs, [VM] * len(outs), scratch, flops, limit)

    side_rows = pltpu.VMEM((2, experts // 2, dirs * slots, width), BF)
    sems = pltpu.SemaphoreType.DMA
    carried = (experts // 2, 2, slots, dirs * width + LANES)

    (x_send,) = kernel("packx", pack_body, [packed], (count_rows, acts[0]), work)
    x_own = dispatch(x_send).reshape(sided.shape)
    wgo = mirror(wg)
    (g_send,) = kernel("packg", pack_scaled_body, [packed], (count_rows, probs[0], out_grad[0]), work)
    g_own = dispatch(g_send).reshape(sided.shape)
    wuo = mirror(wu)
    wdo = mirror(wd)
    x_other = swap(x_own)
    g_other = swap(g_own)
    act, act_t, silu, slope, x_send_t, x_keep_t = kernel(
        "hidden",
        hidden_body,
        [
            shape((total, hidden), BF),
            shape((hidden, total), BF),
            shape((total, hidden), F32),
            shape((total, hidden), F32),
            shape((width, total), BF),
            shape((width, total), BF),
        ],
        (x_own, x_other, wg, wgo, wu, wuo),
        4 * one,
        (0, 1),
        (side_rows, side_rows, sems((4,))),
    )
    (down_send,) = kernel(
        "down",
        down_body,
        [shape((hidden, width), BF)],
        (g_own, g_other, act_t),
        one,
        (0, 1),
        (side_rows, sems((2,))),
    )
    down_got = mirror(down_send)
    d, prob, row_send = kernel(
        "slope",
        slope_body,
        [shape((total, 2 * hidden), BF), shape((total, LANES), F32), shape(carried, BF)],
        (g_own, g_other, wd, wdo, act, silu, slope, wg, wgo, wu, wuo),
        4 * one,
        (0, 1),
        (side_rows, side_rows, sems((4,))),
    )
    row_got = swap(row_send)
    (grad_send,) = kernel(
        "gradsend", grad_send_body, [shape((2, width, hidden), BF)], (x_send_t, d), 2 * one
    )
    grad_got = mirror(grad_send)
    row_keep, grad_keep, down_keep = kernel(
        "keep",
        keep_body,
        [shape(carried, F32), shape((2, width, hidden), F32), shape((hidden, width), F32)],
        (g_own, g_other, x_keep_t, act_t, d, prob, wg, wgo, wu, wuo),
        5 * one,
        (0, 1),
        (side_rows, sems((2,))),
    )
    row_sum = (row_keep + row_got.astype(F32)).astype(BF).reshape(experts, *carried[2:])
    row_back = dispatch(row_sum)
    act_grad, prob_grad = kernel(
        "unpack",
        unpack_body,
        [shape((dirs, rows, width), BF), shape((dirs, rows), BF)],
        (count_rows, probs[0], row_back),
        work,
        (2,),
        (pltpu.VMEM(row_back.shape, BF), sems(())),
    )
    return (
        act_grad[None],
        prob_grad[None],
        settle(grad_keep[0], grad_got[0]),
        settle(grad_keep[1], grad_got[1]),
        settle(down_keep, down_got),
    )


def solution(mesh):
    return jax.shard_map(
        on_device,
        mesh=mesh,
        in_specs=(
            P("pipe", None, "expert", "tensor"),
            P("pipe", None, "expert", "tensor"),
            P("pipe", None, "expert"),
            P("pipe", None, "expert", None),
            P("pipe", "expert", None, "tensor"),
            P("pipe", "expert", None, "tensor"),
            P("pipe", "expert", "tensor", None),
        ),
        out_specs=(
            P("pipe", None, "expert", "tensor"),
            P("pipe", None, "expert"),
            P("pipe", "expert", None, "tensor"),
            P("pipe", "expert", None, "tensor"),
            P("pipe", "expert", "tensor", None),
        ),
        check_vma=False,
    )
```

```python
import jax
import jax.numpy as jnp
from jax import lax
from jax.experimental import pallas as pl
from jax.experimental.pallas import tpu as pltpu
from jax.sharding import PartitionSpec as P


BF = jnp.bfloat16
F32 = jnp.float32
VM = pl.BlockSpec(memory_space=pltpu.VMEM)
ANY = pl.BlockSpec(memory_space=pl.ANY)
LANES = 128


def dot(a, b, ca, cb):
    return lax.dot_general(a, b, (((ca,), (cb,)), ((), ())), preferred_element_type=F32)


def call(body, outs, args, in_specs, out_specs, scratch=(), flops=0, limit=None):
    moved = sum(a.size * a.dtype.itemsize for a in (*args, *outs))
    return pl.pallas_call(
        body,
        out_shape=tuple(outs),
        in_specs=in_specs,
        out_specs=tuple(out_specs),
        scratch_shapes=scratch,
        compiler_params=pltpu.CompilerParams(vmem_limit_bytes=limit),
        cost_estimate=pl.CostEstimate(flops=flops, bytes_accessed=moved, transcendentals=0),
    )(*args)


def shape(dims, kind):
    return jax.ShapeDtypeStruct(dims, kind)


def slot_choice(count_row, slots, rows):
    experts = count_row.shape[1]
    total = experts * slots
    owner = lax.broadcasted_iota(jnp.int32, (total, experts), 0) // slots
    expert = lax.broadcasted_iota(jnp.int32, (total, experts), 1)
    count = jnp.sum(jnp.where(expert == owner, count_row, 0), axis=1, keepdims=True)
    start = jnp.sum(jnp.where(expert < owner, count_row, 0), axis=1, keepdims=True)
    place = lax.broadcasted_iota(jnp.int32, (total, 1), 0) % slots
    target = jnp.where(place < count, start + place, -1)
    return lax.broadcasted_iota(jnp.int32, (total, rows), 1) == target


def pack_body(counts_ref, values_ref, out_ref):
    dirs, rows, width = values_ref.shape
    experts, _, slots, _ = out_ref.shape
    for d in range(dirs):
        mask = slot_choice(counts_ref[d : d + 1, :], slots, rows)
        packed = dot(mask.astype(BF), values_ref[d], 1, 0).astype(BF)
        out_ref[:, d] = packed.reshape(experts, slots, width)


def pack_scaled_body(counts_ref, probs_ref, values_ref, out_ref):
    dirs, rows, width = values_ref.shape
    experts, _, slots, _ = out_ref.shape
    for d in range(dirs):
        mask = slot_choice(counts_ref[d : d + 1, :], slots, rows)
        weight = jnp.where(mask, probs_ref[d : d + 1, :].astype(F32), 0.0).astype(BF)
        packed = dot(weight, values_ref[d], 1, 0).astype(BF)
        out_ref[:, d] = packed.reshape(experts, slots, width)


def unpack_body(counts_ref, probs_ref, filled, out_ref, prob_ref, slots_ref, sem):
    copy = pltpu.make_async_copy(filled, slots_ref, sem)
    copy.start()
    experts, slots, _ = slots_ref.shape
    dirs, rows, width = out_ref.shape
    masks = [
        slot_choice(counts_ref[d : d + 1, :], slots, rows).astype(BF) for d in range(dirs)
    ]
    copy.wait()
    terms = slots_ref[:, :, dirs * width :].reshape(experts * slots, LANES)
    for d in range(dirs):
        part = slots_ref[:, :, d * width : (d + 1) * width].reshape(experts * slots, width)
        out_ref[d] = dot(masks[d], part, 0, 0).astype(BF)
        found = dot(terms, masks[d], 0, 0)[d : d + 1, :]
        prob_ref[d : d + 1, :] = (found / probs_ref[d : d + 1, :].astype(F32)).astype(BF)


def half_index():
    return lax.axis_index("pipe") // (lax.axis_size("pipe") // 2)


def keeps_low():
    half = half_index()
    group = (lax.axis_index("tensor") + lax.axis_index("expert")) % 2
    return half == group


def row_copies(own, other, low, high, sems):
    return [
        pltpu.make_async_copy(own.at[:, 0], low.at[0], sems.at[0]),
        pltpu.make_async_copy(other.at[:, 1], low.at[1], sems.at[1]),
        pltpu.make_async_copy(other.at[:, 0], high.at[0], sems.at[2]),
        pltpu.make_async_copy(own.at[:, 1], high.at[1], sems.at[3]),
    ]


def flat(ref):
    sides, blocks, rows, width = ref.shape
    return ref[...].reshape(sides * blocks * rows, width)


def weight_sides(same, own_ref, other_ref):
    own, other = (own_ref[...], other_ref[...])
    return (jnp.where(same, own, other), jnp.where(same, other, own))


def hidden_body(
    own, other, wg, wgo, wu, wuo, act_ref, act_t_ref, silu_ref, slope_ref, keep_ref, low, high, sems
):
    copies = row_copies(own, other, low, high, sems)
    for c in copies:
        c.start()
    same = keeps_low()
    wga, wgb = weight_sides(same, wg, wgo)
    wua, wub = weight_sides(same, wu, wuo)
    for c in copies:
        c.wait()
    xa, xb = (flat(low), flat(high))
    gate = dot(xa, wga, 1, 0) + dot(xb, wgb, 1, 0)
    up = dot(xa, wua, 1, 0) + dot(xb, wub, 1, 0)
    sigma = jax.nn.sigmoid(gate)
    silu = gate * sigma
    act = (silu * up).astype(BF)
    act_ref[...] = act
    act_t_ref[...] = act.T
    silu_ref[...] = silu
    slope_ref[...] = up * (sigma * (1.0 + gate * (1.0 - sigma)))
    keep_ref[...] = jnp.where(same, xa, xb).T


def half_copies(own, other, wanted_low, buffer, sems):
    @pl.when(wanted_low)
    def _():
        pltpu.make_async_copy(own.at[:, 0], buffer.at[0], sems.at[0]).start()
        pltpu.make_async_copy(other.at[:, 1], buffer.at[1], sems.at[1]).start()

    @pl.when(jnp.logical_not(wanted_low))
    def _():
        pltpu.make_async_copy(other.at[:, 0], buffer.at[0], sems.at[0]).start()
        pltpu.make_async_copy(own.at[:, 1], buffer.at[1], sems.at[1]).start()

    return [
        pltpu.make_async_copy(own.at[:, 0], buffer.at[0], sems.at[0]),
        pltpu.make_async_copy(own.at[:, 1], buffer.at[1], sems.at[1]),
    ]


def down_body(own, other, act_t, down_ref, half, sems):
    for c in half_copies(own, other, jnp.logical_not(keeps_low()), half, sems):
        c.wait()
    down_ref[...] = dot(act_t[...], flat(half), 1, 0).astype(BF)


def row_terms(d, gate_sides, up_sides, prob, out_ref, swapped):
    blocks, _, slots, lanes = out_ref.shape
    width = gate_sides[0].shape[0]
    dirs = lanes // width
    half = blocks * dirs * slots
    hidden = gate_sides[0].shape[1]
    lane = lax.broadcasted_iota(jnp.int32, (blocks, slots, LANES), 2)
    for side in range(2):
        use = side ^ swapped
        part = d[side * half : (side + 1) * half]
        term = dot(part[:, :hidden], gate_sides[use], 1, 1) + dot(part[:, hidden:], up_sides[use], 1, 1)
        term = term.astype(out_ref.dtype).reshape(blocks, dirs, slots, width)
        spread = jnp.broadcast_to(prob[side * half : (side + 1) * half], (half, LANES))
        spread = spread.reshape(blocks, dirs, slots, LANES)
        extra = jnp.zeros((blocks, slots, LANES), F32)
        for k in range(dirs):
            out_ref[:, side, :, k * width : (k + 1) * width] = term[:, k]
            extra = jnp.where(lane == k, spread[:, k], extra)
        out_ref[:, side, :, dirs * width :] = extra.astype(out_ref.dtype)


def slope_body(
    own, other, wd, wdo, act, silu, slope, wg, wgo, wu, wuo, d_ref, prob_ref, row_ref, low, high, sems
):
    copies = row_copies(own, other, low, high, sems)
    for c in copies:
        c.start()
    same = keeps_low()
    wda, wdb = weight_sides(same, wd, wdo)
    for c in copies:
        c.wait()
    back = dot(flat(low), wda, 1, 1) + dot(flat(high), wdb, 1, 1)
    d_gate = (back * slope[...]).astype(BF)
    d_up = (back * silu[...]).astype(BF)
    d = jnp.concatenate([d_gate, d_up], axis=1)
    d_ref[...] = d
    prob = jnp.sum(act[...].astype(F32) * back, axis=1, keepdims=True)
    prob_ref[...] = jnp.broadcast_to(prob, prob_ref.shape)
    row_terms(d, weight_sides(same, wg, wgo), weight_sides(same, wu, wuo), prob, row_ref, 1)


def piece_body(counts_ref, values_ref, other_ref, out_ref):
    rows = other_ref.shape[0]
    experts = counts_ref.shape[1]
    straight = lax.axis_index("tensor") != half_index()
    out_ref[0:rows] = jnp.where(straight, values_ref[0], other_ref[...])
    out_ref[rows:] = jnp.zeros((out_ref.shape[0] - rows, out_ref.shape[1]), BF)
    count = jnp.where(straight, counts_ref[0:1, :], counts_ref[1:2, :])
    padded = jnp.broadcast_to(count.astype(F32), (out_ref.shape[0] - rows, experts))
    out_ref[rows:, 0:experts] = padded.astype(BF)


def pack_piece_body(piece_ref, out_ref):
    experts, slots, width = out_ref.shape
    rows = slots * experts // 2
    count = piece_ref[rows:, :].astype(F32)[0:1, 0:experts].astype(jnp.int32)
    mask = slot_choice(count, slots, rows)
    packed = dot(mask.astype(BF), piece_ref[0:rows, :], 1, 0).astype(BF)
    out_ref[...] = packed.reshape(experts, slots, width)


def turn_body(own, other, out_ref, buffer, sems):
    d = 1 - keeps_low().astype(jnp.int32)
    copies = [
        pltpu.make_async_copy(own.at[:, 0], buffer.at[0, :, d], sems.at[0]),
        pltpu.make_async_copy(other.at[:, 0], buffer.at[0, :, 1 - d], sems.at[1]),
        pltpu.make_async_copy(own.at[:, 1], buffer.at[1, :, 1 - d], sems.at[2]),
        pltpu.make_async_copy(other.at[:, 1], buffer.at[1, :, d], sems.at[3]),
    ]
    for c in copies:
        c.start()
    for c in copies:
        c.wait()
    out_ref[...] = buffer[...].reshape(out_ref.shape[1], out_ref.shape[0]).T


def final_body(x_t, d, keep, gate_ref, up_ref):
    both = dot(x_t[...], d[...], 1, 0)
    hidden = gate_ref.shape[1]
    gate_ref[...] = (keep[0] + both[:, :hidden]).astype(BF)
    up_ref[...] = (keep[1] + both[:, hidden:]).astype(BF)


def keep_body(
    own, other, x_t, act_t, d, prob, wg, wgo, wu, wuo, row_ref, grad_ref, down_ref, half, sems
):
    same = keeps_low()
    waits = half_copies(own, other, same, half, sems)
    row_terms(
        d[...], weight_sides(same, wg, wgo), weight_sides(same, wu, wuo), prob[:, 0:1], row_ref, 0
    )
    both = dot(x_t[...], d[...], 1, 0)
    hidden = grad_ref.shape[2]
    grad_ref[0] = both[:, :hidden]
    grad_ref[1] = both[:, hidden:]
    for c in waits:
        c.wait()
    down_ref[...] = dot(act_t[...], flat(half), 1, 0)


def dispatch(array):
    experts = lax.axis_size("expert")
    groups = [[2 * e + (e + g) % 2 for e in range(experts)] for g in range(2)]
    return lax.all_to_all(
        array, ("expert", "tensor"), 0, 0, axis_index_groups=groups, tiled=True
    )


def settle(keep, arrived):
    return (keep + arrived.astype(F32)).astype(BF)[None, None]


def on_device(acts, out_grad, probs, counts, w_gate, w_up, w_down):
    experts = lax.axis_size("expert")
    pipes = lax.axis_size("pipe")
    dirs, rows, width = acts.shape[1:]
    slots = 2 * rows // experts
    total = dirs * experts * slots
    hidden = w_gate.shape[3]
    wg, wu, wd = (w_gate[0, 0], w_up[0, 0], w_down[0, 0])
    count_rows = counts[0, :, 0, :]
    packed = shape((experts, dirs, slots, width), BF)
    sided = shape((experts // 2, 2, dirs * slots, width), BF)
    work = 2 * dirs * experts * slots * rows * width
    one = 2 * total * width * hidden

    def mirror(array):
        return lax.ppermute(array, "pipe", [(i, (i + pipes // 2) % pipes) for i in range(pipes)])

    def swap(array):
        return lax.ppermute(array, "tensor", [(0, 1), (1, 0)])

    late = ("hidden", "down", "slope", "keep", "turn", "final", "unpack")

    def kernel(name, body, outs, args, flops, in_place=(), scratch=()):
        limit = 24 * 1024 * 1024 if name in late else None
        specs = [ANY if i in in_place else VM for i in range(len(args))]
        return call(body, outs, args, specs, [VM] * len(outs), scratch, flops, limit)

    side_rows = pltpu.VMEM((2, experts // 2, dirs * slots, width), BF)
    sems = pltpu.SemaphoreType.DMA
    carried = (experts // 2, 2, slots, dirs * width + LANES)

    (x_send,) = kernel("packx", pack_body, [packed], (count_rows, acts[0]), work)
    x_own = dispatch(x_send).reshape(sided.shape)
    wgo = mirror(wg)
    (g_send,) = kernel("packg", pack_scaled_body, [packed], (count_rows, probs[0], out_grad[0]), work)
    g_own = dispatch(g_send).reshape(sided.shape)
    wuo = mirror(wu)
    x_second = swap(acts[0, 1])
    (piece,) = kernel(
        "piece", piece_body, [shape((rows + 16, width), BF)], (count_rows, acts[0], x_second), 0
    )
    piece_got = mirror(piece)
    (m_send,) = kernel("packm", pack_piece_body, [shape((experts, slots, width), BF)], (piece_got,), work // 4)
    m_own = dispatch(m_send).reshape(experts // 2, 2, slots, width)
    m_other = swap(m_own)
    wdo = mirror(wd)
    x_other = swap(x_own)
    g_other = swap(g_own)
    act, act_t, silu, slope, x_keep_t = kernel(
        "hidden",
        hidden_body,
        [
            shape((total, hidden), BF),
            shape((hidden, total), BF),
            shape((total, hidden), F32),
            shape((total, hidden), F32),
            shape((width, total), BF),
        ],
        (x_own, x_other, wg, wgo, wu, wuo),
        4 * one,
        (0, 1),
        (side_rows, side_rows, sems((4,))),
    )
    (down_send,) = kernel(
        "down",
        down_body,
        [shape((hidden, width), BF)],
        (g_own, g_other, act_t),
        one,
        (0, 1),
        (side_rows, sems((2,))),
    )
    down_got = mirror(down_send)
    d, prob, row_send = kernel(
        "slope",
        slope_body,
        [shape((total, 2 * hidden), BF), shape((total, LANES), F32), shape(carried, BF)],
        (g_own, g_other, wd, wdo, act, silu, slope, wg, wgo, wu, wuo),
        4 * one,
        (0, 1),
        (side_rows, side_rows, sems((4,))),
    )
    row_got = swap(row_send)
    d_got = mirror(d)
    (m_t,) = kernel(
        "turn",
        turn_body,
        [shape((width, total), BF)],
        (m_own, m_other),
        0,
        (0, 1),
        (pltpu.VMEM((2, experts // 2, dirs, slots, width), BF), sems((4,))),
    )
    row_keep, grad_keep, down_keep = kernel(
        "keep",
        keep_body,
        [shape(carried, F32), shape((2, width, hidden), F32), shape((hidden, width), F32)],
        (g_own, g_other, x_keep_t, act_t, d, prob, wg, wgo, wu, wuo),
        5 * one,
        (0, 1),
        (side_rows, sems((2,))),
    )
    gate_grad, up_grad = kernel(
        "final",
        final_body,
        [shape((width, hidden), BF), shape((width, hidden), BF)],
        (m_t, d_got, grad_keep),
        2 * one,
    )
    row_sum = (row_keep + row_got.astype(F32)).astype(BF).reshape(experts, *carried[2:])
    row_back = dispatch(row_sum)
    act_grad, prob_grad = kernel(
        "unpack",
        unpack_body,
        [shape((dirs, rows, width), BF), shape((dirs, rows), BF)],
        (count_rows, probs[0], row_back),
        work,
        (2,),
        (pltpu.VMEM(row_back.shape, BF), sems(())),
    )
    return (
        act_grad[None],
        prob_grad[None],
        gate_grad[None, None],
        up_grad[None, None],
        settle(down_keep, down_got),
    )


def solution(mesh):
    return jax.shard_map(
        on_device,
        mesh=mesh,
        in_specs=(
            P("pipe", None, "expert", "tensor"),
            P("pipe", None, "expert", "tensor"),
            P("pipe", None, "expert"),
            P("pipe", None, "expert", None),
            P("pipe", "expert", None, "tensor"),
            P("pipe", "expert", None, "tensor"),
            P("pipe", "expert", "tensor", None),
        ),
        out_specs=(
            P("pipe", None, "expert", "tensor"),
            P("pipe", None, "expert"),
            P("pipe", "expert", None, "tensor"),
            P("pipe", "expert", None, "tensor"),
            P("pipe", "expert", "tensor", None),
        ),
        check_vma=False,
    )
```

```python
import jax
import jax.numpy as jnp
from jax import lax
from jax.experimental import pallas as pl
from jax.experimental.pallas import tpu as pltpu
from jax.sharding import PartitionSpec as P


BF = jnp.bfloat16
F32 = jnp.float32
VM = pl.BlockSpec(memory_space=pltpu.VMEM)
ANY = pl.BlockSpec(memory_space=pl.ANY)
LANES = 128


def dot(a, b, ca, cb):
    return lax.dot_general(a, b, (((ca,), (cb,)), ((), ())), preferred_element_type=F32)


def call(body, outs, args, in_specs, out_specs, scratch=(), flops=0, limit=None):
    moved = sum(a.size * a.dtype.itemsize for a in (*args, *outs))
    return pl.pallas_call(
        body,
        out_shape=tuple(outs),
        in_specs=in_specs,
        out_specs=tuple(out_specs),
        scratch_shapes=scratch,
        compiler_params=pltpu.CompilerParams(vmem_limit_bytes=limit),
        cost_estimate=pl.CostEstimate(flops=flops, bytes_accessed=moved, transcendentals=0),
    )(*args)


def shape(dims, kind):
    return jax.ShapeDtypeStruct(dims, kind)


def slot_choice(count_row, slots, rows):
    experts = count_row.shape[1]
    total = experts * slots
    owner = lax.broadcasted_iota(jnp.int32, (total, experts), 0) // slots
    expert = lax.broadcasted_iota(jnp.int32, (total, experts), 1)
    count = jnp.sum(jnp.where(expert == owner, count_row, 0), axis=1, keepdims=True)
    start = jnp.sum(jnp.where(expert < owner, count_row, 0), axis=1, keepdims=True)
    place = lax.broadcasted_iota(jnp.int32, (total, 1), 0) % slots
    target = jnp.where(place < count, start + place, -1)
    return lax.broadcasted_iota(jnp.int32, (total, rows), 1) == target


def pack_body(counts_ref, values_ref, out_ref):
    dirs, rows, width = values_ref.shape
    experts, _, slots, _ = out_ref.shape
    for d in range(dirs):
        mask = slot_choice(counts_ref[d : d + 1, :], slots, rows)
        packed = dot(mask.astype(BF), values_ref[d], 1, 0).astype(BF)
        out_ref[:, d] = packed.reshape(experts, slots, width)


def pack_scaled_body(counts_ref, probs_ref, values_ref, out_ref):
    dirs, rows, width = values_ref.shape
    experts, _, slots, _ = out_ref.shape
    for d in range(dirs):
        mask = slot_choice(counts_ref[d : d + 1, :], slots, rows)
        weight = jnp.where(mask, probs_ref[d : d + 1, :].astype(F32), 0.0).astype(BF)
        packed = dot(weight, values_ref[d], 1, 0).astype(BF)
        out_ref[:, d] = packed.reshape(experts, slots, width)


def unpack_body(counts_ref, probs_ref, first, second, out_ref, prob_ref, first_ref, second_ref, sems):
    copies = [
        pltpu.make_async_copy(first, first_ref, sems.at[0]),
        pltpu.make_async_copy(second, second_ref, sems.at[1]),
    ]
    for c in copies:
        c.start()
    experts, slots, width = second_ref.shape
    dirs, rows, _ = out_ref.shape
    masks = [
        slot_choice(counts_ref[d : d + 1, :], slots, rows).astype(BF) for d in range(dirs)
    ]
    for c in copies:
        c.wait()
    terms = first_ref[:, :, width:].reshape(experts * slots, LANES)
    for d, ref in enumerate((first_ref, second_ref)):
        part = ref[:, :, :width].reshape(experts * slots, width)
        out_ref[d] = dot(masks[d], part, 0, 0).astype(BF)
        found = dot(terms, masks[d], 0, 0)[d : d + 1, :]
        prob_ref[d : d + 1, :] = (found / probs_ref[d : d + 1, :].astype(F32)).astype(BF)


def half_index():
    return lax.axis_index("pipe") // (lax.axis_size("pipe") // 2)


def keeps_low():
    half = half_index()
    group = (lax.axis_index("tensor") + lax.axis_index("expert")) % 2
    return half == group


def row_copies(own, other, low, high, sems):
    return [
        pltpu.make_async_copy(own.at[:, 0], low.at[0], sems.at[0]),
        pltpu.make_async_copy(other.at[:, 1], low.at[1], sems.at[1]),
        pltpu.make_async_copy(other.at[:, 0], high.at[0], sems.at[2]),
        pltpu.make_async_copy(own.at[:, 1], high.at[1], sems.at[3]),
    ]


def flat(ref):
    sides, blocks, rows, width = ref.shape
    return ref[...].reshape(sides * blocks * rows, width)


def weight_sides(same, own_ref, other_ref):
    own, other = (own_ref[...], other_ref[...])
    return (jnp.where(same, own, other), jnp.where(same, other, own))


def hidden_body(
    own, other, wg, wgo, wu, wuo, act_ref, act_t_ref, silu_ref, slope_ref, keep_ref, low, high, sems
):
    copies = row_copies(own, other, low, high, sems)
    for c in copies:
        c.start()
    same = keeps_low()
    wga, wgb = weight_sides(same, wg, wgo)
    wua, wub = weight_sides(same, wu, wuo)
    for c in copies:
        c.wait()
    xa, xb = (flat(low), flat(high))
    gate = dot(xa, wga, 1, 0) + dot(xb, wgb, 1, 0)
    up = dot(xa, wua, 1, 0) + dot(xb, wub, 1, 0)
    sigma = jax.nn.sigmoid(gate)
    silu = gate * sigma
    act = (silu * up).astype(BF)
    act_ref[...] = act
    act_t_ref[...] = act.T
    silu_ref[...] = silu
    slope_ref[...] = up * (sigma * (1.0 + gate * (1.0 - sigma)))
    keep_ref[...] = jnp.where(same, xa, xb).T


def half_copies(own, other, wanted_low, buffer, sems):
    @pl.when(wanted_low)
    def _():
        pltpu.make_async_copy(own.at[:, 0], buffer.at[0], sems.at[0]).start()
        pltpu.make_async_copy(other.at[:, 1], buffer.at[1], sems.at[1]).start()

    @pl.when(jnp.logical_not(wanted_low))
    def _():
        pltpu.make_async_copy(other.at[:, 0], buffer.at[0], sems.at[0]).start()
        pltpu.make_async_copy(own.at[:, 1], buffer.at[1], sems.at[1]).start()

    return [
        pltpu.make_async_copy(own.at[:, 0], buffer.at[0], sems.at[0]),
        pltpu.make_async_copy(own.at[:, 1], buffer.at[1], sems.at[1]),
    ]


def down_body(own, other, act_t, down_ref, half, sems):
    for c in half_copies(own, other, jnp.logical_not(keeps_low()), half, sems):
        c.wait()
    down_ref[...] = dot(act_t[...], flat(half), 1, 0).astype(BF)


def row_terms(d, gate_sides, up_sides, prob, first_ref, second_ref, swapped):
    blocks, _, slots, width = second_ref.shape
    half = 2 * blocks * slots
    hidden = gate_sides[0].shape[1]
    lane = lax.broadcasted_iota(jnp.int32, (blocks, slots, LANES), 2)
    kind = second_ref.dtype
    for side in range(2):
        use = side ^ swapped
        part = d[side * half : (side + 1) * half]
        term = dot(part[:, :hidden], gate_sides[use], 1, 1) + dot(part[:, hidden:], up_sides[use], 1, 1)
        term = term.astype(kind).reshape(blocks, 2, slots, width)
        first_ref[:, side, :, :width] = term[:, 0]
        second_ref[:, side] = term[:, 1]
        spread = jnp.broadcast_to(prob[side * half : (side + 1) * half], (half, LANES))
        spread = spread.reshape(blocks, 2, slots, LANES)
        extra = jnp.where(lane == 0, spread[:, 0], jnp.where(lane == 1, spread[:, 1], 0.0))
        first_ref[:, side, :, width:] = extra.astype(kind)


def slope_body(
    own, other, wd, wdo, act, silu, slope, wg, wgo, wu, wuo, d_ref, prob_ref, first_ref, second_ref, low, high, sems
):
    copies = row_copies(own, other, low, high, sems)
    for c in copies:
        c.start()
    same = keeps_low()
    wda, wdb = weight_sides(same, wd, wdo)
    for c in copies:
        c.wait()
    back = dot(flat(low), wda, 1, 1) + dot(flat(high), wdb, 1, 1)
    d_gate = (back * slope[...]).astype(BF)
    d_up = (back * silu[...]).astype(BF)
    d = jnp.concatenate([d_gate, d_up], axis=1)
    d_ref[...] = d
    prob = jnp.sum(act[...].astype(F32) * back, axis=1, keepdims=True)
    prob_ref[...] = jnp.broadcast_to(prob, prob_ref.shape)
    row_terms(d, weight_sides(same, wg, wgo), weight_sides(same, wu, wuo), prob, first_ref, second_ref, 1)


def piece_body(counts_ref, values_ref, other_ref, out_ref):
    rows = other_ref.shape[0]
    experts = counts_ref.shape[1]
    straight = lax.axis_index("tensor") != half_index()
    out_ref[0:rows] = jnp.where(straight, values_ref[0], other_ref[...])
    out_ref[rows:] = jnp.zeros((out_ref.shape[0] - rows, out_ref.shape[1]), BF)
    count = jnp.where(straight, counts_ref[0:1, :], counts_ref[1:2, :])
    padded = jnp.broadcast_to(count.astype(F32), (out_ref.shape[0] - rows, experts))
    out_ref[rows:, 0:experts] = padded.astype(BF)


def pack_piece_body(piece_ref, out_ref):
    experts, slots, width = out_ref.shape
    rows = slots * experts // 2
    count = piece_ref[rows:, :].astype(F32)[0:1, 0:experts].astype(jnp.int32)
    mask = slot_choice(count, slots, rows)
    packed = dot(mask.astype(BF), piece_ref[0:rows, :], 1, 0).astype(BF)
    out_ref[...] = packed.reshape(experts, slots, width)


def turn_body(own, other, out_ref, buffer, sems):
    d = 1 - keeps_low().astype(jnp.int32)
    copies = [
        pltpu.make_async_copy(own.at[:, 0], buffer.at[0, :, d], sems.at[0]),
        pltpu.make_async_copy(other.at[:, 0], buffer.at[0, :, 1 - d], sems.at[1]),
        pltpu.make_async_copy(own.at[:, 1], buffer.at[1, :, 1 - d], sems.at[2]),
        pltpu.make_async_copy(other.at[:, 1], buffer.at[1, :, d], sems.at[3]),
    ]
    for c in copies:
        c.start()
    for c in copies:
        c.wait()
    out_ref[...] = buffer[...].reshape(out_ref.shape[1], out_ref.shape[0]).T


def final_body(x_t, d, keep, gate_ref, up_ref):
    both = dot(x_t[...], d[...], 1, 0)
    hidden = gate_ref.shape[1]
    gate_ref[...] = (keep[0] + both[:, :hidden]).astype(BF)
    up_ref[...] = (keep[1] + both[:, hidden:]).astype(BF)


def row_keep_body(d, prob, wg, wgo, wu, wuo, first_ref, second_ref):
    same = keeps_low()
    row_terms(
        d[...],
        weight_sides(same, wg, wgo),
        weight_sides(same, wu, wuo),
        prob[:, 0:1],
        first_ref,
        second_ref,
        0,
    )


def keep_body(own, other, x_t, act_t, d, grad_ref, down_ref, half, sems):
    waits = half_copies(own, other, keeps_low(), half, sems)
    both = dot(x_t[...], d[...], 1, 0)
    hidden = grad_ref.shape[2]
    grad_ref[0] = both[:, :hidden]
    grad_ref[1] = both[:, hidden:]
    for c in waits:
        c.wait()
    down_ref[...] = dot(act_t[...], flat(half), 1, 0)


def dispatch(array):
    experts = lax.axis_size("expert")
    groups = [[2 * e + (e + g) % 2 for e in range(experts)] for g in range(2)]
    return lax.all_to_all(
        array, ("expert", "tensor"), 0, 0, axis_index_groups=groups, tiled=True
    )


def settle(keep, arrived):
    return (keep + arrived.astype(F32)).astype(BF)[None, None]


def on_device(acts, out_grad, probs, counts, w_gate, w_up, w_down):
    experts = lax.axis_size("expert")
    pipes = lax.axis_size("pipe")
    dirs, rows, width = acts.shape[1:]
    slots = 2 * rows // experts
    total = dirs * experts * slots
    hidden = w_gate.shape[3]
    wg, wu, wd = (w_gate[0, 0], w_up[0, 0], w_down[0, 0])
    count_rows = counts[0, :, 0, :]
    packed = shape((experts, dirs, slots, width), BF)
    sided = shape((experts // 2, 2, dirs * slots, width), BF)
    work = 2 * dirs * experts * slots * rows * width
    one = 2 * total * width * hidden

    def mirror(array):
        return lax.ppermute(array, "pipe", [(i, (i + pipes // 2) % pipes) for i in range(pipes)])

    def swap(array):
        return lax.ppermute(array, "tensor", [(0, 1), (1, 0)])

    late = ("hidden", "down", "slope", "rowkeep", "keep", "turn", "final", "unpack")

    def kernel(name, body, outs, args, flops, in_place=(), scratch=()):
        limit = 24 * 1024 * 1024 if name in late else None
        specs = [ANY if i in in_place else VM for i in range(len(args))]
        return call(body, outs, args, specs, [VM] * len(outs), scratch, flops, limit)

    side_rows = pltpu.VMEM((2, experts // 2, dirs * slots, width), BF)
    sems = pltpu.SemaphoreType.DMA
    firsts = (experts // 2, 2, slots, width + LANES)
    seconds = (experts // 2, 2, slots, width)

    (x_send,) = kernel("packx", pack_body, [packed], (count_rows, acts[0]), work)
    x_own = dispatch(x_send).reshape(sided.shape)
    wgo = mirror(wg)
    (g_send,) = kernel("packg", pack_scaled_body, [packed], (count_rows, probs[0], out_grad[0]), work)
    g_own = dispatch(g_send).reshape(sided.shape)
    wuo = mirror(wu)
    x_second = swap(acts[0, 1])
    (piece,) = kernel(
        "piece", piece_body, [shape((rows + 16, width), BF)], (count_rows, acts[0], x_second), 0
    )
    piece_got = mirror(piece)
    (m_send,) = kernel("packm", pack_piece_body, [shape((experts, slots, width), BF)], (piece_got,), work // 4)
    m_own = dispatch(m_send).reshape(experts // 2, 2, slots, width)
    m_other = swap(m_own)
    wdo = mirror(wd)
    x_other = swap(x_own)
    g_other = swap(g_own)
    act, act_t, silu, slope, x_keep_t = kernel(
        "hidden",
        hidden_body,
        [
            shape((total, hidden), BF),
            shape((hidden, total), BF),
            shape((total, hidden), F32),
            shape((total, hidden), F32),
            shape((width, total), BF),
        ],
        (x_own, x_other, wg, wgo, wu, wuo),
        4 * one,
        (0, 1),
        (side_rows, side_rows, sems((4,))),
    )
    (down_send,) = kernel(
        "down",
        down_body,
        [shape((hidden, width), BF)],
        (g_own, g_other, act_t),
        one,
        (0, 1),
        (side_rows, sems((2,))),
    )
    down_got = mirror(down_send)
    d, prob, first_send, second_send = kernel(
        "slope",
        slope_body,
        [
            shape((total, 2 * hidden), BF),
            shape((total, LANES), F32),
            shape(firsts, BF),
            shape(seconds, BF),
        ],
        (g_own, g_other, wd, wdo, act, silu, slope, wg, wgo, wu, wuo),
        4 * one,
        (0, 1),
        (side_rows, side_rows, sems((4,))),
    )
    first_got = swap(first_send)
    second_got = swap(second_send)
    first_keep, second_keep = kernel(
        "rowkeep",
        row_keep_body,
        [shape(firsts, F32), shape(seconds, F32)],
        (d, prob, wg, wgo, wu, wuo),
        2 * one,
    )
    d_got = mirror(d)
    (m_t,) = kernel(
        "turn",
        turn_body,
        [shape((width, total), BF)],
        (m_own, m_other),
        0,
        (0, 1),
        (pltpu.VMEM((2, experts // 2, dirs, slots, width), BF), sems((4,))),
    )
    grad_keep, down_keep = kernel(
        "keep",
        keep_body,
        [shape((2, width, hidden), F32), shape((hidden, width), F32)],
        (g_own, g_other, x_keep_t, act_t, d),
        3 * one,
        (0, 1),
        (side_rows, sems((2,))),
    )
    gate_grad, up_grad = kernel(
        "final",
        final_body,
        [shape((width, hidden), BF), shape((width, hidden), BF)],
        (m_t, d_got, grad_keep),
        2 * one,
    )

    def returned(keep, got):
        summed = (keep + got.astype(F32)).astype(BF).reshape(experts, *keep.shape[2:])
        return dispatch(summed)

    first_back = returned(first_keep, first_got)
    second_back = returned(second_keep, second_got)
    act_grad, prob_grad = kernel(
        "unpack",
        unpack_body,
        [shape((dirs, rows, width), BF), shape((dirs, rows), BF)],
        (count_rows, probs[0], first_back, second_back),
        work,
        (2, 3),
        (pltpu.VMEM(first_back.shape, BF), pltpu.VMEM(second_back.shape, BF), sems((2,))),
    )
    return (
        act_grad[None],
        prob_grad[None],
        gate_grad[None, None],
        up_grad[None, None],
        settle(down_keep, down_got),
    )


def solution(mesh):
    return jax.shard_map(
        on_device,
        mesh=mesh,
        in_specs=(
            P("pipe", None, "expert", "tensor"),
            P("pipe", None, "expert", "tensor"),
            P("pipe", None, "expert"),
            P("pipe", None, "expert", None),
            P("pipe", "expert", None, "tensor"),
            P("pipe", "expert", None, "tensor"),
            P("pipe", "expert", "tensor", None),
        ),
        out_specs=(
            P("pipe", None, "expert", "tensor"),
            P("pipe", None, "expert"),
            P("pipe", "expert", None, "tensor"),
            P("pipe", "expert", None, "tensor"),
            P("pipe", "expert", "tensor", None),
        ),
        check_vma=False,
    )
```

```python
import jax
import jax.numpy as jnp
from jax import lax
from jax.experimental import pallas as pl
from jax.experimental.pallas import tpu as pltpu
from jax.sharding import PartitionSpec as P


BF = jnp.bfloat16
F32 = jnp.float32
VM = pl.BlockSpec(memory_space=pltpu.VMEM)
ANY = pl.BlockSpec(memory_space=pl.ANY)
LANES = 128


def dot(a, b, ca, cb):
    return lax.dot_general(a, b, (((ca,), (cb,)), ((), ())), preferred_element_type=F32)


def call(body, outs, args, in_specs, out_specs, scratch=(), flops=0, limit=None):
    moved = sum(a.size * a.dtype.itemsize for a in (*args, *outs))
    return pl.pallas_call(
        body,
        out_shape=tuple(outs),
        in_specs=in_specs,
        out_specs=tuple(out_specs),
        scratch_shapes=scratch,
        compiler_params=pltpu.CompilerParams(vmem_limit_bytes=limit),
        cost_estimate=pl.CostEstimate(flops=flops, bytes_accessed=moved, transcendentals=0),
    )(*args)


def shape(dims, kind):
    return jax.ShapeDtypeStruct(dims, kind)


def slot_choice(count_row, slots, rows):
    experts = count_row.shape[1]
    total = experts * slots
    owner = lax.broadcasted_iota(jnp.int32, (total, experts), 0) // slots
    expert = lax.broadcasted_iota(jnp.int32, (total, experts), 1)
    count = jnp.sum(jnp.where(expert == owner, count_row, 0), axis=1, keepdims=True)
    start = jnp.sum(jnp.where(expert < owner, count_row, 0), axis=1, keepdims=True)
    place = lax.broadcasted_iota(jnp.int32, (total, 1), 0) % slots
    target = jnp.where(place < count, start + place, -1)
    return lax.broadcasted_iota(jnp.int32, (total, rows), 1) == target


def pack_body(counts_ref, values_ref, out_ref):
    dirs, rows, width = values_ref.shape
    experts, _, slots, _ = out_ref.shape
    for d in range(dirs):
        mask = slot_choice(counts_ref[d : d + 1, :], slots, rows)
        packed = dot(mask.astype(BF), values_ref[d], 1, 0).astype(BF)
        out_ref[:, d] = packed.reshape(experts, slots, width)


def pack_scaled_body(counts_ref, probs_ref, values_ref, out_ref):
    dirs, rows, width = values_ref.shape
    experts, _, slots, _ = out_ref.shape
    for d in range(dirs):
        mask = slot_choice(counts_ref[d : d + 1, :], slots, rows)
        weight = jnp.where(mask, probs_ref[d : d + 1, :].astype(F32), 0.0).astype(BF)
        packed = dot(weight, values_ref[d], 1, 0).astype(BF)
        out_ref[:, d] = packed.reshape(experts, slots, width)


def unpack_body(counts_ref, probs_ref, first, second, out_ref, prob_ref, first_ref, second_ref, sems):
    copies = [
        pltpu.make_async_copy(first, first_ref, sems.at[0]),
        pltpu.make_async_copy(second, second_ref, sems.at[1]),
    ]
    for c in copies:
        c.start()
    experts, slots, width = second_ref.shape
    dirs, rows, _ = out_ref.shape
    masks = [
        slot_choice(counts_ref[d : d + 1, :], slots, rows).astype(BF) for d in range(dirs)
    ]
    for c in copies:
        c.wait()
    terms = first_ref[:, :, width:].reshape(experts * slots, LANES)
    for d, ref in enumerate((first_ref, second_ref)):
        part = ref[:, :, :width].reshape(experts * slots, width)
        out_ref[d] = dot(masks[d], part, 0, 0).astype(BF)
        found = dot(terms, masks[d], 0, 0)[d : d + 1, :]
        prob_ref[d : d + 1, :] = (found / probs_ref[d : d + 1, :].astype(F32)).astype(BF)


def half_index():
    return lax.axis_index("pipe") // (lax.axis_size("pipe") // 2)


def keeps_low():
    half = half_index()
    group = (lax.axis_index("tensor") + lax.axis_index("expert")) % 2
    return half == group


def row_copies(own, other, low, high, sems):
    return [
        pltpu.make_async_copy(own.at[:, 0], low.at[0], sems.at[0]),
        pltpu.make_async_copy(other.at[:, 1], low.at[1], sems.at[1]),
        pltpu.make_async_copy(other.at[:, 0], high.at[0], sems.at[2]),
        pltpu.make_async_copy(own.at[:, 1], high.at[1], sems.at[3]),
    ]


def flat(ref):
    sides, blocks, rows, width = ref.shape
    return ref[...].reshape(sides * blocks * rows, width)


def weight_sides(same, own_ref, other_ref):
    own, other = (own_ref[...], other_ref[...])
    return (jnp.where(same, own, other), jnp.where(same, other, own))


def hidden_body(
    own, other, wg, wgo, wu, wuo, act_ref, act_t_ref, silu_ref, slope_ref, keep_ref, low, high, sems
):
    copies = row_copies(own, other, low, high, sems)
    for c in copies:
        c.start()
    same = keeps_low()
    wga, wgb = weight_sides(same, wg, wgo)
    wua, wub = weight_sides(same, wu, wuo)
    for c in copies:
        c.wait()
    xa, xb = (flat(low), flat(high))
    gate = dot(xa, wga, 1, 0) + dot(xb, wgb, 1, 0)
    up = dot(xa, wua, 1, 0) + dot(xb, wub, 1, 0)
    sigma = jax.nn.sigmoid(gate)
    silu = gate * sigma
    act = (silu * up).astype(BF)
    act_ref[...] = act
    act_t_ref[...] = act.T
    silu_ref[...] = silu
    slope_ref[...] = up * (sigma * (1.0 + gate * (1.0 - sigma)))
    keep_ref[...] = jnp.where(same, xa, xb).T


def half_copies(own, other, wanted_low, buffer, sems):
    @pl.when(wanted_low)
    def _():
        pltpu.make_async_copy(own.at[:, 0], buffer.at[0], sems.at[0]).start()
        pltpu.make_async_copy(other.at[:, 1], buffer.at[1], sems.at[1]).start()

    @pl.when(jnp.logical_not(wanted_low))
    def _():
        pltpu.make_async_copy(other.at[:, 0], buffer.at[0], sems.at[0]).start()
        pltpu.make_async_copy(own.at[:, 1], buffer.at[1], sems.at[1]).start()

    return [
        pltpu.make_async_copy(own.at[:, 0], buffer.at[0], sems.at[0]),
        pltpu.make_async_copy(own.at[:, 1], buffer.at[1], sems.at[1]),
    ]


def down_body(own, other, act_t, down_ref, half, sems):
    for c in half_copies(own, other, jnp.logical_not(keeps_low()), half, sems):
        c.wait()
    down_ref[...] = dot(act_t[...], flat(half), 1, 0).astype(BF)


def row_terms(d, gate_sides, up_sides, prob, first_ref, second_ref, swapped):
    blocks, _, slots, width = second_ref.shape
    half = 2 * blocks * slots
    hidden = gate_sides[0].shape[1]
    lane = lax.broadcasted_iota(jnp.int32, (blocks, slots, LANES), 2)
    kind = second_ref.dtype
    for side in range(2):
        use = side ^ swapped
        part = d[side * half : (side + 1) * half]
        term = dot(part[:, :hidden], gate_sides[use], 1, 1) + dot(part[:, hidden:], up_sides[use], 1, 1)
        term = term.astype(kind).reshape(blocks, 2, slots, width)
        first_ref[:, side, :, :width] = term[:, 0]
        second_ref[:, side] = term[:, 1]
        spread = jnp.broadcast_to(prob[side * half : (side + 1) * half], (half, LANES))
        spread = spread.reshape(blocks, 2, slots, LANES)
        extra = jnp.where(lane == 0, spread[:, 0], jnp.where(lane == 1, spread[:, 1], 0.0))
        first_ref[:, side, :, width:] = extra.astype(kind)


def slope_body(
    own, other, wd, wdo, act, silu, slope, wg, wgo, wu, wuo, d_ref, prob_ref, first_ref, second_ref, low, high, sems
):
    copies = row_copies(own, other, low, high, sems)
    for c in copies:
        c.start()
    same = keeps_low()
    wda, wdb = weight_sides(same, wd, wdo)
    for c in copies:
        c.wait()
    back = dot(flat(low), wda, 1, 1) + dot(flat(high), wdb, 1, 1)
    d_gate = (back * slope[...]).astype(BF)
    d_up = (back * silu[...]).astype(BF)
    d = jnp.concatenate([d_gate, d_up], axis=1)
    d_ref[...] = d
    prob = jnp.sum(act[...].astype(F32) * back, axis=1, keepdims=True)
    prob_ref[...] = jnp.broadcast_to(prob, prob_ref.shape)
    row_terms(d, weight_sides(same, wg, wgo), weight_sides(same, wu, wuo), prob, first_ref, second_ref, 1)


def piece_body(counts_ref, values_ref, other_ref, out_ref):
    rows = other_ref.shape[0]
    experts = counts_ref.shape[1]
    straight = lax.axis_index("tensor") != half_index()
    out_ref[0:rows] = jnp.where(straight, values_ref[0], other_ref[...])
    out_ref[rows:] = jnp.zeros((out_ref.shape[0] - rows, out_ref.shape[1]), BF)
    count = jnp.where(straight, counts_ref[0:1, :], counts_ref[1:2, :])
    padded = jnp.broadcast_to(count.astype(F32), (out_ref.shape[0] - rows, experts))
    out_ref[rows:, 0:experts] = padded.astype(BF)


def pack_piece_body(piece_ref, out_ref):
    experts, slots, width = out_ref.shape
    rows = slots * experts // 2
    count = piece_ref[rows:, :].astype(F32)[0:1, 0:experts].astype(jnp.int32)
    mask = slot_choice(count, slots, rows)
    packed = dot(mask.astype(BF), piece_ref[0:rows, :], 1, 0).astype(BF)
    out_ref[...] = packed.reshape(experts, slots, width)


def turn_body(own, other, out_ref, buffer, sems):
    d = 1 - keeps_low().astype(jnp.int32)
    copies = [
        pltpu.make_async_copy(own.at[:, 0], buffer.at[0, :, d], sems.at[0]),
        pltpu.make_async_copy(other.at[:, 0], buffer.at[0, :, 1 - d], sems.at[1]),
        pltpu.make_async_copy(own.at[:, 1], buffer.at[1, :, 1 - d], sems.at[2]),
        pltpu.make_async_copy(other.at[:, 1], buffer.at[1, :, d], sems.at[3]),
    ]
    for c in copies:
        c.start()
    for c in copies:
        c.wait()
    out_ref[...] = buffer[...].reshape(out_ref.shape[1], out_ref.shape[0]).T


def final_body(x_t, d, keep, gate_ref, up_ref):
    both = dot(x_t[...], d[...], 1, 0)
    hidden = gate_ref.shape[1]
    gate_ref[...] = (keep[0] + both[:, :hidden]).astype(BF)
    up_ref[...] = (keep[1] + both[:, hidden:]).astype(BF)


def row_keep_body(d, prob, wg, wgo, wu, wuo, first_ref, second_ref):
    same = keeps_low()
    row_terms(
        d[...],
        weight_sides(same, wg, wgo),
        weight_sides(same, wu, wuo),
        prob[:, 0:1],
        first_ref,
        second_ref,
        0,
    )


def down_keep_body(own, other, act_t, down_ref, half, sems):
    for c in half_copies(own, other, keeps_low(), half, sems):
        c.wait()
    down_ref[...] = dot(act_t[...], flat(half), 1, 0)


def grad_keep_body(x_t, d, grad_ref):
    both = dot(x_t[...], d[...], 1, 0)
    hidden = grad_ref.shape[2]
    grad_ref[0] = both[:, :hidden]
    grad_ref[1] = both[:, hidden:]


def dispatch(array):
    experts = lax.axis_size("expert")
    groups = [[2 * e + (e + g) % 2 for e in range(experts)] for g in range(2)]
    return lax.all_to_all(
        array, ("expert", "tensor"), 0, 0, axis_index_groups=groups, tiled=True
    )


def settle(keep, arrived):
    return (keep + arrived.astype(F32)).astype(BF)[None, None]


def on_device(acts, out_grad, probs, counts, w_gate, w_up, w_down):
    experts = lax.axis_size("expert")
    pipes = lax.axis_size("pipe")
    dirs, rows, width = acts.shape[1:]
    slots = 2 * rows // experts
    total = dirs * experts * slots
    hidden = w_gate.shape[3]
    wg, wu, wd = (w_gate[0, 0], w_up[0, 0], w_down[0, 0])
    count_rows = counts[0, :, 0, :]
    packed = shape((experts, dirs, slots, width), BF)
    sided = shape((experts // 2, 2, dirs * slots, width), BF)
    work = 2 * dirs * experts * slots * rows * width
    one = 2 * total * width * hidden

    def mirror(array):
        return lax.ppermute(array, "pipe", [(i, (i + pipes // 2) % pipes) for i in range(pipes)])

    def swap(array):
        return lax.ppermute(array, "tensor", [(0, 1), (1, 0)])

    late = ("hidden", "down", "slope", "rowkeep", "downkeep", "gradkeep", "turn", "final", "unpack")

    def kernel(name, body, outs, args, flops, in_place=(), scratch=()):
        limit = 24 * 1024 * 1024 if name in late else None
        specs = [ANY if i in in_place else VM for i in range(len(args))]
        return call(body, outs, args, specs, [VM] * len(outs), scratch, flops, limit)

    side_rows = pltpu.VMEM((2, experts // 2, dirs * slots, width), BF)
    sems = pltpu.SemaphoreType.DMA
    firsts = (experts // 2, 2, slots, width + LANES)
    seconds = (experts // 2, 2, slots, width)

    (x_send,) = kernel("packx", pack_body, [packed], (count_rows, acts[0]), work)
    x_own = dispatch(x_send).reshape(sided.shape)
    wgo = mirror(wg)
    (g_send,) = kernel("packg", pack_scaled_body, [packed], (count_rows, probs[0], out_grad[0]), work)
    g_own = dispatch(g_send).reshape(sided.shape)
    wuo = mirror(wu)
    x_second = swap(acts[0, 1])
    (piece,) = kernel(
        "piece", piece_body, [shape((rows + 16, width), BF)], (count_rows, acts[0], x_second), 0
    )
    piece_got = mirror(piece)
    (m_send,) = kernel("packm", pack_piece_body, [shape((experts, slots, width), BF)], (piece_got,), work // 4)
    m_own = dispatch(m_send).reshape(experts // 2, 2, slots, width)
    m_other = swap(m_own)
    wdo = mirror(wd)
    x_other = swap(x_own)
    g_other = swap(g_own)
    act, act_t, silu, slope, x_keep_t = kernel(
        "hidden",
        hidden_body,
        [
            shape((total, hidden), BF),
            shape((hidden, total), BF),
            shape((total, hidden), F32),
            shape((total, hidden), F32),
            shape((width, total), BF),
        ],
        (x_own, x_other, wg, wgo, wu, wuo),
        4 * one,
        (0, 1),
        (side_rows, side_rows, sems((4,))),
    )
    (down_send,) = kernel(
        "down",
        down_body,
        [shape((hidden, width), BF)],
        (g_own, g_other, act_t),
        one,
        (0, 1),
        (side_rows, sems((2,))),
    )
    down_got = mirror(down_send)
    d, prob, first_send, second_send = kernel(
        "slope",
        slope_body,
        [
            shape((total, 2 * hidden), BF),
            shape((total, LANES), F32),
            shape(firsts, BF),
            shape(seconds, BF),
        ],
        (g_own, g_other, wd, wdo, act, silu, slope, wg, wgo, wu, wuo),
        4 * one,
        (0, 1),
        (side_rows, side_rows, sems((4,))),
    )
    first_got = swap(first_send)
    second_got = swap(second_send)
    first_keep, second_keep = kernel(
        "rowkeep",
        row_keep_body,
        [shape(firsts, F32), shape(seconds, F32)],
        (d, prob, wg, wgo, wu, wuo),
        2 * one,
    )
    d_got = mirror(d)
    (m_t,) = kernel(
        "turn",
        turn_body,
        [shape((width, total), BF)],
        (m_own, m_other),
        0,
        (0, 1),
        (pltpu.VMEM((2, experts // 2, dirs, slots, width), BF), sems((4,))),
    )
    (down_keep,) = kernel(
        "downkeep",
        down_keep_body,
        [shape((hidden, width), F32)],
        (g_own, g_other, act_t),
        one,
        (0, 1),
        (side_rows, sems((2,))),
    )
    (grad_keep,) = kernel(
        "gradkeep", grad_keep_body, [shape((2, width, hidden), F32)], (x_keep_t, d), 2 * one
    )
    gate_grad, up_grad = kernel(
        "final",
        final_body,
        [shape((width, hidden), BF), shape((width, hidden), BF)],
        (m_t, d_got, grad_keep),
        2 * one,
    )

    def returned(keep, got):
        summed = (keep + got.astype(F32)).astype(BF).reshape(experts, *keep.shape[2:])
        return dispatch(summed)

    first_back = returned(first_keep, first_got)
    second_back = returned(second_keep, second_got)
    act_grad, prob_grad = kernel(
        "unpack",
        unpack_body,
        [shape((dirs, rows, width), BF), shape((dirs, rows), BF)],
        (count_rows, probs[0], first_back, second_back),
        work,
        (2, 3),
        (pltpu.VMEM(first_back.shape, BF), pltpu.VMEM(second_back.shape, BF), sems((2,))),
    )
    return (
        act_grad[None],
        prob_grad[None],
        gate_grad[None, None],
        up_grad[None, None],
        settle(down_keep, down_got),
    )


def solution(mesh):
    return jax.shard_map(
        on_device,
        mesh=mesh,
        in_specs=(
            P("pipe", None, "expert", "tensor"),
            P("pipe", None, "expert", "tensor"),
            P("pipe", None, "expert"),
            P("pipe", None, "expert", None),
            P("pipe", "expert", None, "tensor"),
            P("pipe", "expert", None, "tensor"),
            P("pipe", "expert", "tensor", None),
        ),
        out_specs=(
            P("pipe", None, "expert", "tensor"),
            P("pipe", None, "expert"),
            P("pipe", "expert", None, "tensor"),
            P("pipe", "expert", None, "tensor"),
            P("pipe", "expert", "tensor", None),
        ),
        check_vma=False,
    )
```

```python
import jax
import jax.numpy as jnp
from jax import lax
from jax.experimental import pallas as pl
from jax.experimental.pallas import tpu as pltpu
from jax.sharding import PartitionSpec as P


BF = jnp.bfloat16
F32 = jnp.float32
VM = pl.BlockSpec(memory_space=pltpu.VMEM)
ANY = pl.BlockSpec(memory_space=pl.ANY)
LANES = 128


def dot(a, b, ca, cb):
    return lax.dot_general(a, b, (((ca,), (cb,)), ((), ())), preferred_element_type=F32)


def call(body, outs, args, in_specs, out_specs, scratch=(), flops=0, limit=None):
    moved = sum(a.size * a.dtype.itemsize for a in (*args, *outs))
    return pl.pallas_call(
        body,
        out_shape=tuple(outs),
        in_specs=in_specs,
        out_specs=tuple(out_specs),
        scratch_shapes=scratch,
        compiler_params=pltpu.CompilerParams(vmem_limit_bytes=limit),
        cost_estimate=pl.CostEstimate(flops=flops, bytes_accessed=moved, transcendentals=0),
    )(*args)


def shape(dims, kind):
    return jax.ShapeDtypeStruct(dims, kind)


def slot_choice(count_row, slots, rows, offset=0):
    experts = count_row.shape[1]
    total = experts * slots
    owner = lax.broadcasted_iota(jnp.int32, (total, experts), 0) // slots
    expert = lax.broadcasted_iota(jnp.int32, (total, experts), 1)
    count = jnp.sum(jnp.where(expert == owner, count_row, 0), axis=1, keepdims=True)
    start = jnp.sum(jnp.where(expert < owner, count_row, 0), axis=1, keepdims=True)
    place = lax.broadcasted_iota(jnp.int32, (total, 1), 0) % slots + offset
    target = jnp.where((place >= 0) & (place < count), start + place, -1)
    return lax.broadcasted_iota(jnp.int32, (total, rows), 1) == target


def pack_body(counts_ref, values_ref, out_ref):
    dirs, rows, width = values_ref.shape
    experts, _, slots, _ = out_ref.shape
    for d in range(dirs):
        mask = slot_choice(counts_ref[d : d + 1, :], slots, rows)
        packed = dot(mask.astype(BF), values_ref[d], 1, 0).astype(BF)
        out_ref[:, d] = packed.reshape(experts, slots, width)


def pack_scaled_body(counts_ref, probs_ref, values_ref, out_ref):
    dirs, rows, width = values_ref.shape
    experts, _, slots, _ = out_ref.shape
    for d in range(dirs):
        mask = slot_choice(counts_ref[d : d + 1, :], slots, rows)
        weight = jnp.where(mask, probs_ref[d : d + 1, :].astype(F32), 0.0).astype(BF)
        packed = dot(weight, values_ref[d], 1, 0).astype(BF)
        out_ref[:, d] = packed.reshape(experts, slots, width)


def unpack_body(counts_ref, probs_ref, first, second, out_ref, prob_ref, first_ref, second_ref, sems):
    copies = [
        pltpu.make_async_copy(first, first_ref, sems.at[0]),
        pltpu.make_async_copy(second, second_ref, sems.at[1]),
    ]
    for c in copies:
        c.start()
    experts, rest, width = second_ref.shape
    few = first_ref.shape[1]
    dirs, rows, _ = out_ref.shape

    def mask(d, slots, offset):
        return slot_choice(counts_ref[d : d + 1, :], slots, rows, offset)

    early = mask(0, few, 0).astype(BF)
    place = lax.broadcasted_iota(jnp.int32, (experts * rest, 1), 0) % rest
    late = (mask(0, rest, few) & (place < few)).astype(BF)
    other = mask(1, rest, -few).astype(BF)
    halves = [[mask(d, few, part * few).astype(BF) for part in range(2)] for d in range(dirs)]
    for c in copies:
        c.wait()
    head = first_ref[:, :, :width].reshape(experts * few, width)
    tail = second_ref[...].reshape(experts * rest, width)
    terms = first_ref[:, :, width:].reshape(experts * few, LANES)
    out_ref[0] = (dot(early, head, 0, 0) + dot(late, tail, 0, 0)).astype(BF)
    out_ref[1] = dot(other, tail, 0, 0).astype(BF)
    for d in range(dirs):
        found = sum(dot(terms, halves[d][part], 0, 0)[2 * d + part :][:1] for part in range(2))
        prob_ref[d : d + 1, :] = (found / probs_ref[d : d + 1, :].astype(F32)).astype(BF)


def half_index():
    return lax.axis_index("pipe") // (lax.axis_size("pipe") // 2)


def keeps_low():
    half = half_index()
    group = (lax.axis_index("tensor") + lax.axis_index("expert")) % 2
    return half == group


def row_copies(own, other, low, high, sems):
    return [
        pltpu.make_async_copy(own.at[:, 0], low.at[0], sems.at[0]),
        pltpu.make_async_copy(other.at[:, 1], low.at[1], sems.at[1]),
        pltpu.make_async_copy(other.at[:, 0], high.at[0], sems.at[2]),
        pltpu.make_async_copy(own.at[:, 1], high.at[1], sems.at[3]),
    ]


def flat(ref):
    sides, blocks, rows, width = ref.shape
    return ref[...].reshape(sides * blocks * rows, width)


def weight_sides(same, own_ref, other_ref):
    own, other = (own_ref[...], other_ref[...])
    return (jnp.where(same, own, other), jnp.where(same, other, own))


def hidden_body(
    own, other, wg, wgo, wu, wuo, act_ref, act_t_ref, silu_ref, slope_ref, keep_ref, low, high, sems
):
    copies = row_copies(own, other, low, high, sems)
    for c in copies:
        c.start()
    same = keeps_low()
    wga, wgb = weight_sides(same, wg, wgo)
    wua, wub = weight_sides(same, wu, wuo)
    for c in copies:
        c.wait()
    xa, xb = (flat(low), flat(high))
    gate = dot(xa, wga, 1, 0) + dot(xb, wgb, 1, 0)
    up = dot(xa, wua, 1, 0) + dot(xb, wub, 1, 0)
    sigma = jax.nn.sigmoid(gate)
    silu = gate * sigma
    act = (silu * up).astype(BF)
    act_ref[...] = act
    act_t_ref[...] = act.T
    silu_ref[...] = silu
    slope_ref[...] = up * (sigma * (1.0 + gate * (1.0 - sigma)))
    keep_ref[...] = jnp.where(same, xa, xb).T


def half_copies(own, other, wanted_low, buffer, sems):
    @pl.when(wanted_low)
    def _():
        pltpu.make_async_copy(own.at[:, 0], buffer.at[0], sems.at[0]).start()
        pltpu.make_async_copy(other.at[:, 1], buffer.at[1], sems.at[1]).start()

    @pl.when(jnp.logical_not(wanted_low))
    def _():
        pltpu.make_async_copy(other.at[:, 0], buffer.at[0], sems.at[0]).start()
        pltpu.make_async_copy(own.at[:, 1], buffer.at[1], sems.at[1]).start()

    return [
        pltpu.make_async_copy(own.at[:, 0], buffer.at[0], sems.at[0]),
        pltpu.make_async_copy(own.at[:, 1], buffer.at[1], sems.at[1]),
    ]


def down_body(own, other, act_t, down_ref, half, sems):
    for c in half_copies(own, other, jnp.logical_not(keeps_low()), half, sems):
        c.wait()
    down_ref[...] = dot(act_t[...], flat(half), 1, 0).astype(BF)


def row_terms(d, gate_sides, up_sides, prob, first_ref, second_ref, swapped):
    blocks, _, few, _ = first_ref.shape
    width = second_ref.shape[3]
    slots = 2 * few
    half = 2 * blocks * slots
    hidden = gate_sides[0].shape[1]
    lane = lax.broadcasted_iota(jnp.int32, (blocks, few, LANES), 2)
    kind = second_ref.dtype
    for side in range(2):
        use = side ^ swapped
        part = d[side * half : (side + 1) * half]
        term = dot(part[:, :hidden], gate_sides[use], 1, 1) + dot(part[:, hidden:], up_sides[use], 1, 1)
        term = term.reshape(blocks, 2 * slots, width)
        first_ref[:, side, :, :width] = term[:, :few].astype(kind)
        second_ref[:, side] = term[:, few:].astype(kind)
        spread = jnp.broadcast_to(prob[side * half : (side + 1) * half], (half, LANES))
        spread = spread.reshape(blocks, 2 * slots, LANES)
        extra = jnp.zeros((blocks, few, LANES), F32)
        for k in range(4):
            extra = jnp.where(lane == k, spread[:, k * few : (k + 1) * few], extra)
        first_ref[:, side, :, width:] = extra.astype(kind)


def slope_body(
    own, other, wd, wdo, act, silu, slope, wg, wgo, wu, wuo, d_ref, prob_ref, first_ref, second_ref, low, high, sems
):
    copies = row_copies(own, other, low, high, sems)
    for c in copies:
        c.start()
    same = keeps_low()
    wda, wdb = weight_sides(same, wd, wdo)
    for c in copies:
        c.wait()
    back = dot(flat(low), wda, 1, 1) + dot(flat(high), wdb, 1, 1)
    d_gate = (back * slope[...]).astype(BF)
    d_up = (back * silu[...]).astype(BF)
    d = jnp.concatenate([d_gate, d_up], axis=1)
    d_ref[...] = d
    prob = jnp.sum(act[...].astype(F32) * back, axis=1, keepdims=True)
    prob_ref[...] = jnp.broadcast_to(prob, prob_ref.shape)
    row_terms(d, weight_sides(same, wg, wgo), weight_sides(same, wu, wuo), prob, first_ref, second_ref, 1)


def piece_body(counts_ref, values_ref, other_ref, out_ref):
    rows = other_ref.shape[0]
    experts = counts_ref.shape[1]
    straight = lax.axis_index("tensor") != half_index()
    out_ref[0:rows] = jnp.where(straight, values_ref[0], other_ref[...])
    out_ref[rows:] = jnp.zeros((out_ref.shape[0] - rows, out_ref.shape[1]), BF)
    count = jnp.where(straight, counts_ref[0:1, :], counts_ref[1:2, :])
    padded = jnp.broadcast_to(count.astype(F32), (out_ref.shape[0] - rows, experts))
    out_ref[rows:, 0:experts] = padded.astype(BF)


def pack_piece_body(piece_ref, out_ref):
    experts, slots, width = out_ref.shape
    rows = slots * experts // 2
    count = piece_ref[rows:, :].astype(F32)[0:1, 0:experts].astype(jnp.int32)
    mask = slot_choice(count, slots, rows)
    packed = dot(mask.astype(BF), piece_ref[0:rows, :], 1, 0).astype(BF)
    out_ref[...] = packed.reshape(experts, slots, width)


def turn_body(own, other, out_ref, buffer, sems):
    d = 1 - keeps_low().astype(jnp.int32)
    copies = [
        pltpu.make_async_copy(own.at[:, 0], buffer.at[0, :, d], sems.at[0]),
        pltpu.make_async_copy(other.at[:, 0], buffer.at[0, :, 1 - d], sems.at[1]),
        pltpu.make_async_copy(own.at[:, 1], buffer.at[1, :, 1 - d], sems.at[2]),
        pltpu.make_async_copy(other.at[:, 1], buffer.at[1, :, d], sems.at[3]),
    ]
    for c in copies:
        c.start()
    for c in copies:
        c.wait()
    out_ref[...] = buffer[...].reshape(out_ref.shape[1], out_ref.shape[0]).T


def final_body(x_t, d, keep, gate_ref, up_ref):
    both = dot(x_t[...], d[...], 1, 0)
    hidden = gate_ref.shape[1]
    gate_ref[...] = (keep[0] + both[:, :hidden]).astype(BF)
    up_ref[...] = (keep[1] + both[:, hidden:]).astype(BF)


def row_keep_body(d, prob, wg, wgo, wu, wuo, first_ref, second_ref):
    same = keeps_low()
    row_terms(
        d[...],
        weight_sides(same, wg, wgo),
        weight_sides(same, wu, wuo),
        prob[:, 0:1],
        first_ref,
        second_ref,
        0,
    )


def down_keep_body(own, other, act_t, down_ref, half, sems):
    for c in half_copies(own, other, keeps_low(), half, sems):
        c.wait()
    down_ref[...] = dot(act_t[...], flat(half), 1, 0)


def grad_keep_body(x_t, d, grad_ref):
    both = dot(x_t[...], d[...], 1, 0)
    hidden = grad_ref.shape[2]
    grad_ref[0] = both[:, :hidden]
    grad_ref[1] = both[:, hidden:]


def dispatch(array):
    experts = lax.axis_size("expert")
    groups = [[2 * e + (e + g) % 2 for e in range(experts)] for g in range(2)]
    return lax.all_to_all(
        array, ("expert", "tensor"), 0, 0, axis_index_groups=groups, tiled=True
    )


def settle(keep, arrived):
    return (keep + arrived.astype(F32)).astype(BF)[None, None]


def on_device(acts, out_grad, probs, counts, w_gate, w_up, w_down):
    experts = lax.axis_size("expert")
    pipes = lax.axis_size("pipe")
    dirs, rows, width = acts.shape[1:]
    slots = 2 * rows // experts
    total = dirs * experts * slots
    hidden = w_gate.shape[3]
    wg, wu, wd = (w_gate[0, 0], w_up[0, 0], w_down[0, 0])
    count_rows = counts[0, :, 0, :]
    packed = shape((experts, dirs, slots, width), BF)
    sided = shape((experts // 2, 2, dirs * slots, width), BF)
    work = 2 * dirs * experts * slots * rows * width
    one = 2 * total * width * hidden

    def mirror(array):
        return lax.ppermute(array, "pipe", [(i, (i + pipes // 2) % pipes) for i in range(pipes)])

    def swap(array):
        return lax.ppermute(array, "tensor", [(0, 1), (1, 0)])

    late = ("hidden", "down", "slope", "rowkeep", "downkeep", "gradkeep", "turn", "final", "unpack")

    def kernel(name, body, outs, args, flops, in_place=(), scratch=()):
        limit = 24 * 1024 * 1024 if name in late else None
        specs = [ANY if i in in_place else VM for i in range(len(args))]
        return call(body, outs, args, specs, [VM] * len(outs), scratch, flops, limit)

    side_rows = pltpu.VMEM((2, experts // 2, dirs * slots, width), BF)
    sems = pltpu.SemaphoreType.DMA
    few = slots // 2
    firsts = (experts // 2, 2, few, width + LANES)
    seconds = (experts // 2, 2, dirs * slots - few, width)

    (x_send,) = kernel("packx", pack_body, [packed], (count_rows, acts[0]), work)
    x_own = dispatch(x_send).reshape(sided.shape)
    wgo = mirror(wg)
    (g_send,) = kernel("packg", pack_scaled_body, [packed], (count_rows, probs[0], out_grad[0]), work)
    g_own = dispatch(g_send).reshape(sided.shape)
    wuo = mirror(wu)
    x_second = swap(acts[0, 1])
    (piece,) = kernel(
        "piece", piece_body, [shape((rows + 16, width), BF)], (count_rows, acts[0], x_second), 0
    )
    piece_got = mirror(piece)
    (m_send,) = kernel("packm", pack_piece_body, [shape((experts, slots, width), BF)], (piece_got,), work // 4)
    m_own = dispatch(m_send).reshape(experts // 2, 2, slots, width)
    m_other = swap(m_own)
    wdo = mirror(wd)
    x_other = swap(x_own)
    g_other = swap(g_own)
    act, act_t, silu, slope, x_keep_t = kernel(
        "hidden",
        hidden_body,
        [
            shape((total, hidden), BF),
            shape((hidden, total), BF),
            shape((total, hidden), F32),
            shape((total, hidden), F32),
            shape((width, total), BF),
        ],
        (x_own, x_other, wg, wgo, wu, wuo),
        4 * one,
        (0, 1),
        (side_rows, side_rows, sems((4,))),
    )
    (down_send,) = kernel(
        "down",
        down_body,
        [shape((hidden, width), BF)],
        (g_own, g_other, act_t),
        one,
        (0, 1),
        (side_rows, sems((2,))),
    )
    down_got = mirror(down_send)
    d, prob, first_send, second_send = kernel(
        "slope",
        slope_body,
        [
            shape((total, 2 * hidden), BF),
            shape((total, LANES), F32),
            shape(firsts, BF),
            shape(seconds, BF),
        ],
        (g_own, g_other, wd, wdo, act, silu, slope, wg, wgo, wu, wuo),
        4 * one,
        (0, 1),
        (side_rows, side_rows, sems((4,))),
    )
    first_got = swap(first_send)
    second_got = swap(second_send)
    first_keep, second_keep = kernel(
        "rowkeep",
        row_keep_body,
        [shape(firsts, F32), shape(seconds, F32)],
        (d, prob, wg, wgo, wu, wuo),
        2 * one,
    )
    d_got = mirror(d)
    (m_t,) = kernel(
        "turn",
        turn_body,
        [shape((width, total), BF)],
        (m_own, m_other),
        0,
        (0, 1),
        (pltpu.VMEM((2, experts // 2, dirs, slots, width), BF), sems((4,))),
    )
    (down_keep,) = kernel(
        "downkeep",
        down_keep_body,
        [shape((hidden, width), F32)],
        (g_own, g_other, act_t),
        one,
        (0, 1),
        (side_rows, sems((2,))),
    )
    (grad_keep,) = kernel(
        "gradkeep", grad_keep_body, [shape((2, width, hidden), F32)], (x_keep_t, d), 2 * one
    )
    gate_grad, up_grad = kernel(
        "final",
        final_body,
        [shape((width, hidden), BF), shape((width, hidden), BF)],
        (m_t, d_got, grad_keep),
        2 * one,
    )

    def returned(keep, got):
        summed = (keep + got.astype(F32)).astype(BF).reshape(experts, *keep.shape[2:])
        return dispatch(summed)

    first_back = returned(first_keep, first_got)
    second_back = returned(second_keep, second_got)
    act_grad, prob_grad = kernel(
        "unpack",
        unpack_body,
        [shape((dirs, rows, width), BF), shape((dirs, rows), BF)],
        (count_rows, probs[0], first_back, second_back),
        work,
        (2, 3),
        (pltpu.VMEM(first_back.shape, BF), pltpu.VMEM(second_back.shape, BF), sems((2,))),
    )
    return (
        act_grad[None],
        prob_grad[None],
        gate_grad[None, None],
        up_grad[None, None],
        settle(down_keep, down_got),
    )


def solution(mesh):
    return jax.shard_map(
        on_device,
        mesh=mesh,
        in_specs=(
            P("pipe", None, "expert", "tensor"),
            P("pipe", None, "expert", "tensor"),
            P("pipe", None, "expert"),
            P("pipe", None, "expert", None),
            P("pipe", "expert", None, "tensor"),
            P("pipe", "expert", None, "tensor"),
            P("pipe", "expert", "tensor", None),
        ),
        out_specs=(
            P("pipe", None, "expert", "tensor"),
            P("pipe", None, "expert"),
            P("pipe", "expert", None, "tensor"),
            P("pipe", "expert", None, "tensor"),
            P("pipe", "expert", "tensor", None),
        ),
        check_vma=False,
    )
```
